128 devices in a mesh: ctx: 32 (over y, z, x_lo), ch: 4 (over x_hi, core).
Axes of the slice: x: 4 (x_hi: 2, x_lo: 2; x = x_hi * 2 + x_lo), y: 4, z: 4, core: 2. Of those that a mesh axis runs over, the one named last changes fastest.
Arguments:
- signal: bfloat16 [256, 512, 1024], P('ctx', None, 'ch'), may hold values from -15 to 15
- factor_first: bfloat16 [4, 512, 512], P('ch'), may hold values from -0.25 to 0.25
- factor_second: bfloat16 [4, 256, 256], P('ch'), may hold values from -0.375 to 0.375
- up_weight: bfloat16 [4, 256, 1024], P('ch'), may hold values from -0.375 to 0.375
- down_weight: bfloat16 [4, 1024, 256], P('ch'), may hold values from -0.1875 to 0.1875
- norm_gain: float32 [4, 256], P('ch'), may hold values from 0.1 to 1.9
- cotangent: bfloat16 [512, 256, 1024], P('ctx', None, 'ch'), may hold values from -6 to 6
Outputs:
- layer_out: bfloat16 [512, 256, 1024], P('ctx', None, 'ch')
- grad_signal: bfloat16 [256, 512, 1024], P('ctx', None, 'ch')
- grad_first: float32 [4, 512, 512], P('ch', 'ctx')
- grad_second: float32 [4, 256, 256], P('ch', 'ctx')
- grad_up: float32 [4, 256, 1024], P('ch', 'ctx')
- grad_down: float32 [4, 1024, 256], P('ch', 'ctx')
- grad_gain: float32 [4, 256], P('ch', 'ctx')
The draws below stay inside these ranges and needn't reach their ends.
All inputs are finite; a program needn't handle non-finite values.
Results may differ from the reference program's by a relative error of at most 0.0095.
Values may be sent and summed in bfloat16 or wider, within the bound.
A program may use at most 128 MiB of HBM per device.

```python
import math
import jax
import jax.numpy as jnp
from jax import lax

D = 1024
G = 4
DG = 256
HG = 1024
NB = 512
NA = 256


def draw_signal(key, part):
    noise_key, scale_key = jax.random.split(key)
    channel_ramp = jnp.arange(D, dtype=jnp.float32) / (D - 1)
    values = jax.random.truncated_normal(noise_key, -4.0, 4.0, (NA, NB, D), jnp.float32)
    spread = jax.random.uniform(scale_key, (D,), jnp.float32, 0.0, math.log(4.0))
    scales = 0.3 * jnp.exp(spread + channel_ramp * math.log(3.0))
    return (values * scales).astype(jnp.bfloat16)


def levels(stream_key, extent, cuts, least, high):
    loudness, own = 1.0, jax.random.fold_in(stream_key, 6)
    for axis_at, blocks in cuts:
        draws = jnp.exp(jax.random.uniform(jax.random.fold_in(own, axis_at), (blocks,), jnp.float32, least / len(cuts), high / len(cuts)))
        loudness = loudness * jnp.repeat(draws, extent[axis_at] // blocks).reshape([-1 if axis == axis_at else 1 for axis in range(len(extent))])
    return loudness


def noise(stream_key, dims, width, most, pieces=(), kind=jnp.bfloat16):
    entries = width * jax.random.normal(stream_key, dims, jnp.float32)
    if pieces:
        entries = entries * levels(stream_key, dims, pieces, -0.22, 0.18)
    return jnp.clip(entries, -most, most).astype(kind)


def setup_inputs(seed: int = 0) -> dict:
    key_of = jax.random.split(jax.random.key(seed), 8)
    signal = draw_signal(jax.random.fold_in(key_of[7], 71), 0)
    factor_first = noise(key_of[1], (G, NB, NB), NB ** -0.5, 0.25, ((0, 4),))
    factor_second = noise(key_of[2], (G, NA, NA), NA ** -0.5, 0.375, ((0, 4),))
    up_weight = noise(key_of[3], (G, DG, HG), DG ** -0.5, 0.375, ((0, 4),))
    down_weight = noise(key_of[4], (G, HG, DG), HG ** -0.5, 0.1875, ((0, 4),))
    norm_gain = jnp.clip(1.0 + 0.18 * jax.random.normal(key_of[5], (G, DG), jnp.float32), 0.1, 1.9)
    cotangent = noise(key_of[6], (NB, NA, D), 1.0, 6.0, ((0, 32), (2, 4)))
    return dict(signal=signal, factor_first=factor_first, factor_second=factor_second, up_weight=up_weight, down_weight=down_weight, norm_gain=norm_gain, cotangent=cotangent)


EPSILON = 1e-05

def group_mix(inputs, first_block, second_block):
    values = inputs.astype(jnp.float32)
    first_mix = jnp.einsum('abc,bj->ajc', values, first_block.astype(jnp.float32))
    gate_open = jax.nn.sigmoid(values)
    gated_rows = (first_mix * gate_open).astype(jnp.bfloat16)
    mixed_rows = jnp.einsum('ajc,ai->jic', gated_rows.astype(jnp.float32), second_block.astype(jnp.float32))
    return (first_mix, gate_open, gated_rows, mixed_rows)

def reference(signal, factor_first, factor_second, up_weight, down_weight, norm_gain, cotangent):
    group_width = D // G
    by_group = signal.reshape(NA, NB, G, group_width).transpose(2, 0, 1, 3)
    upstream = cotangent.reshape(NB, NA, G, group_width).transpose(2, 0, 1, 3)
    mixed_all = lax.map(lambda parts: group_mix(parts[0], parts[1], parts[2])[3], (by_group, factor_first, factor_second))
    mean_square = lax.optimization_barrier(jnp.sum(mixed_all * mixed_all, axis=(0, 3))) / D
    inverse = lax.rsqrt(mean_square + EPSILON)[:, :, None]

    def mlp_group(parts):
        mixed_rows, gain_row, up_block, down_block, upstream_rows = parts
        gain_values = gain_row.astype(jnp.float32)
        normed = (mixed_rows * inverse * gain_values).astype(jnp.bfloat16)
        preact = jnp.einsum('jic,ch->jih', normed.astype(jnp.float32), up_block.astype(jnp.float32))
        activation, gelu_back = jax.vjp(jax.nn.gelu, preact)
        act_rows = activation.astype(jnp.bfloat16)
        down_float = down_block.astype(jnp.float32)
        layer_rows = (mixed_rows + jnp.einsum('jih,hc->jic', act_rows.astype(jnp.float32), down_float)).astype(jnp.bfloat16)
        upstream_float = upstream_rows.astype(jnp.float32)
        grad_act = jnp.einsum('jic,hc->jih', upstream_float, down_float)
        grad_pre = gelu_back(grad_act)[0].astype(jnp.bfloat16)
        grad_down = jnp.einsum('jih,jic->hc', act_rows.astype(jnp.float32), upstream_float)
        grad_up = jnp.einsum('jic,jih->ch', normed.astype(jnp.float32), grad_pre.astype(jnp.float32))
        grad_normed = jnp.einsum('jih,ch->jic', grad_pre.astype(jnp.float32), up_block.astype(jnp.float32))
        grad_gain = lax.optimization_barrier(jnp.sum(grad_normed * mixed_rows * inverse, axis=(0, 1)))
        grad_scaled = grad_normed * gain_values
        cross_part = lax.optimization_barrier(jnp.sum(grad_scaled * mixed_rows, axis=2))
        return (layer_rows, grad_down, grad_up, grad_gain, grad_scaled, cross_part)
    layer_groups, grad_downs, grad_ups, grad_gains, scaled_all, cross_parts = lax.map(mlp_group, (mixed_all, norm_gain, up_weight, down_weight, upstream))
    cross = lax.optimization_barrier(jnp.sum(cross_parts, axis=0)) / D

    def back_group(parts):
        inputs, first_block, second_block, mixed_rows, grad_scaled, upstream_rows = parts
        first_mix, gate_open, gated_rows, unused = group_mix(inputs, first_block, second_block)
        grad_mixed = (upstream_rows.astype(jnp.float32) + inverse * grad_scaled - inverse ** 3 * mixed_rows * cross[:, :, None]).astype(jnp.bfloat16)
        grad_second = jnp.einsum('ajc,jic->ai', gated_rows.astype(jnp.float32), grad_mixed.astype(jnp.float32))
        grad_gated = jnp.einsum('jic,ai->ajc', grad_mixed.astype(jnp.float32), second_block.astype(jnp.float32)).astype(jnp.bfloat16)
        gated_float = grad_gated.astype(jnp.float32)
        grad_first_mix = (gated_float * gate_open).astype(jnp.bfloat16)
        grad_gate = gated_float * first_mix * gate_open * (1.0 - gate_open)
        grad_input = (jnp.einsum('ajc,bj->abc', grad_first_mix.astype(jnp.float32), first_block.astype(jnp.float32)) + grad_gate).astype(jnp.bfloat16)
        grad_first = jnp.einsum('abc,ajc->bj', inputs.astype(jnp.float32), grad_first_mix.astype(jnp.float32))
        return (grad_input, grad_first, grad_second)
    grad_inputs, grad_firsts, grad_seconds = lax.map(back_group, (by_group, factor_first, factor_second, mixed_all, scaled_all, upstream))
    grad_scale = (NA * NB) ** (-0.5)
    layer_out = layer_groups.transpose(1, 2, 0, 3).reshape(NB, NA, D)
    grad_signal = grad_inputs.transpose(1, 2, 0, 3).reshape(NA, NB, D)
    return (layer_out, grad_signal, grad_firsts * grad_scale, grad_seconds * grad_scale, grad_ups * grad_scale, grad_downs * grad_scale, grad_gains * grad_scale)
```

```python
import jax
import jax.numpy as jnp
from jax import lax
from jax.sharding import PartitionSpec as P

D = 1024
NB = 512
NA = 256


EPSILON = 1e-05


def transpose_slab(block):
    return lax.all_to_all(block, "ctx", split_axis=1, concat_axis=0, tiled=True)


def channel_total(partial_value):
    return lax.psum(partial_value, "ch")


def shards(signal, factor_first, factor_second, up_weight, down_weight, norm_gain, cotangent):
    groups = factor_first.shape[0]
    group_width = up_weight.shape[1]
    local_rows = signal.shape[0]
    row_count = signal.shape[1]
    inputs = signal.reshape(local_rows, row_count, groups, group_width)
    first_mix = jnp.einsum(
        "abgc,gbj->ajgc", inputs, factor_first, preferred_element_type=jnp.float32
    )
    gate_open = jax.nn.sigmoid(inputs.astype(jnp.float32))
    gated_rows = (first_mix * gate_open).astype(jnp.bfloat16)
    moved_rows = transpose_slab(gated_rows)
    mixed_rows = jnp.einsum(
        "ajgc,gai->jigc", moved_rows, factor_second, preferred_element_type=jnp.float32
    )
    mean_square = channel_total(jnp.sum(mixed_rows * mixed_rows, axis=(2, 3))) / D
    inverse = lax.rsqrt(mean_square + EPSILON)[:, :, None, None]
    gain_rows = norm_gain[None, None]
    normed = (mixed_rows * inverse * gain_rows).astype(jnp.bfloat16)
    preact = jnp.einsum("jigc,gch->jigh", normed, up_weight, preferred_element_type=jnp.float32)
    activation, gelu_back = jax.vjp(jax.nn.gelu, preact)
    act_rows = activation.astype(jnp.bfloat16)
    layer_out = (
        mixed_rows
        + jnp.einsum("jigh,ghc->jigc", act_rows, down_weight, preferred_element_type=jnp.float32)
    ).astype(jnp.bfloat16)
    upstream = cotangent.reshape(mixed_rows.shape)
    grad_act = jnp.einsum(
        "jigc,ghc->jigh", upstream, down_weight, preferred_element_type=jnp.float32
    )
    grad_pre = gelu_back(grad_act)[0].astype(jnp.bfloat16)
    grad_down = jnp.einsum("jigh,jigc->ghc", act_rows, upstream, preferred_element_type=jnp.float32)
    grad_up = jnp.einsum("jigc,jigh->gch", normed, grad_pre, preferred_element_type=jnp.float32)
    grad_normed = jnp.einsum(
        "jigh,gch->jigc", grad_pre, up_weight, preferred_element_type=jnp.float32
    )
    grad_gain = jnp.sum(grad_normed * mixed_rows * inverse, axis=(0, 1))
    grad_scaled = grad_normed * gain_rows
    cross = channel_total(jnp.sum(grad_scaled * mixed_rows, axis=(2, 3))) / D
    grad_mixed = (
        upstream.astype(jnp.float32)
        + inverse * grad_scaled
        - inverse**3 * mixed_rows * cross[:, :, None, None]
    ).astype(jnp.bfloat16)
    grad_second = jnp.einsum(
        "ajgc,jigc->gai", moved_rows, grad_mixed, preferred_element_type=jnp.float32
    )
    grad_moved = jnp.einsum(
        "jigc,gai->jagc", grad_mixed, factor_second, preferred_element_type=jnp.float32
    ).astype(jnp.bfloat16)
    grad_gated = jnp.swapaxes(transpose_slab(grad_moved), 0, 1)
    gated_float = grad_gated.astype(jnp.float32)
    grad_first_mix = (gated_float * gate_open).astype(jnp.bfloat16)
    grad_gate = gated_float * first_mix * gate_open * (1.0 - gate_open)
    grad_input = (
        jnp.einsum(
            "ajgc,gbj->abgc", grad_first_mix, factor_first, preferred_element_type=jnp.float32
        )
        + grad_gate
    ).astype(jnp.bfloat16)
    grad_first = jnp.einsum(
        "abgc,ajgc->gbj", inputs, grad_first_mix, preferred_element_type=jnp.float32
    )
    size = lax.axis_size("ctx")
    partials = (grad_first, grad_second, grad_up, grad_down, grad_gain[:, :, None])
    packed = jnp.concatenate(
        [value[0].reshape(size, -1).astype(jnp.bfloat16) for value in partials], axis=1
    )
    arrived = lax.all_to_all(packed, "ctx", split_axis=0, concat_axis=0, tiled=True)
    total = jnp.sum(arrived.astype(jnp.float32), axis=0)
    summed, at = [], 0
    for value in partials:
        rows = value.shape[1] // size
        count = rows * value.shape[2]
        summed.append(total[at : at + count].reshape(1, rows, value.shape[2]))
        at += count
    summed[4] = summed[4].reshape(1, -1)
    grad_scale = (NA * NB) ** (-0.5)
    return (
        layer_out.reshape(cotangent.shape),
        grad_input.reshape(signal.shape),
        summed[0] * grad_scale,
        summed[1] * grad_scale,
        summed[2] * grad_scale,
        summed[3] * grad_scale,
        summed[4] * grad_scale,
    )


def solution(mesh):
    placed = (
        P("ctx", None, "ch"),
        P("ch", None, None),
        P("ch", None, None),
        P("ch", None, None),
        P("ch", None, None),
        P("ch", None),
        P("ctx", None, "ch"),
    )
    return jax.shard_map(
        shards,
        mesh=mesh,
        in_specs=placed,
        out_specs=(
            P("ctx", None, "ch"),
            P("ctx", None, "ch"),
            P("ch", "ctx", None),
            P("ch", "ctx", None),
            P("ch", "ctx", None),
            P("ch", "ctx", None),
            P("ch", "ctx"),
        ),
        check_vma=False,
    )
```

```python
import functools
import math

import jax
import jax.numpy as jnp
from jax import lax
from jax.experimental import pallas as pl
from jax.experimental.pallas import tpu as pltpu
from jax.sharding import PartitionSpec as P

D = 1024
EPSILON = 1e-05
CHUNKS = 4
LANES = 128
ROWS = 8
HIDDEN = 256
MESH = pl.DeviceIdType.MESH
BF16 = jnp.bfloat16
F32 = jnp.float32
CUBIC = 0.044715
SLOPE = math.sqrt(2.0 / math.pi)


def dot(lhs, rhs):
    return jnp.dot(lhs, rhs, preferred_element_type=F32)


def dot_rows(lhs, rhs):
    return lax.dot_general(lhs, rhs, (((0,), (0,)), ((), ())), preferred_element_type=F32)


def dot_columns(lhs, rhs):
    return lax.dot_general(lhs, rhs, (((1,), (1,)), ((), ())), preferred_element_type=F32)


def lane_blocks(value):
    return [value[..., at : at + LANES] for at in range(0, value.shape[-1], LANES)]


def kernel(
    groups, signal, first, second, up, down, gain, cotangent,
    layer_out, grad_signal, out_first, out_second, out_up, out_down, out_gain,
    first_t, second_t, up_t, down_t, first_mix, stage, send_one, recv_one, moved, mixed_all,
    scaled_all, squares, crosses, inverse_rows, inverse_wide, cross_wide, send_two, recv_two,
    unpacked, acc_up, acc_down, acc_second, acc_first, acc_gain, pack_one, got_one, pack_two,
    got_two, one_send, one_recv, two_send, two_recv, square_send, square_recv, cross_send,
    cross_recv, grad_send, grad_recv,
):
    me = lax.axis_index("ctx")
    channel = lax.axis_index("ch")
    local_a, positions, width = signal.shape
    local_j, rows, _ = cotangent.shape
    hidden = up.shape[1]
    size = rows // local_a
    span = local_j // CHUNKS
    block = stage.shape[1] // local_a - ROWS
    per_block = block // local_j
    blocks = positions // block
    pitch = block + ROWS
    chunk_rows = span * local_a
    halves = width // LANES
    grad_scale = 1.0 / math.sqrt(rows * positions)

    barrier = pltpu.get_barrier_semaphore()

    def greet(k, carry):
        pl.semaphore_signal(
            barrier, inc=1, device_id={"ctx": lax.rem(me + k, size)}, device_id_type=MESH
        )
        return carry

    lax.fori_loop(1, size, greet, 0)
    for k in range(1, groups):
        pl.semaphore_signal(
            barrier, inc=1, device_id={"ch": lax.rem(channel + k, groups)}, device_id_type=MESH
        )

    first_t[...] = first[...].T

    def send_first(target, q):
        part = pl.ds(pl.multiple_of(q * chunk_rows, chunk_rows), chunk_rows)

        @pl.when(target != me)
        def _():
            pltpu.make_async_remote_copy(
                src_ref=send_one.at[target, part],
                dst_ref=recv_one.at[me, part],
                send_sem=one_send,
                recv_sem=one_recv.at[q],
                device_id={"ctx": target},
                device_id_type=MESH,
            ).start()

        @pl.when(target == me)
        def _():
            pltpu.make_async_copy(
                send_one.at[me, part], recv_one.at[me, part], one_recv.at[q]
            ).start()

    def first_block(step, carry):
        at = lax.rem(me // per_block + step, blocks)
        part = pl.ds(pl.multiple_of(at * block, block), block)
        weights = first_t[part, :]
        for a in range(local_a):
            mix = dot(weights, signal[a])
            first_mix[a, part, :] = mix
            gated = mix * lax.logistic(signal[a, part, :].astype(F32))
            for h, piece in enumerate(lane_blocks(gated)):
                stage[h, a * pitch : a * pitch + block, :] = piece

        def turn(k, inner):
            for h in range(halves):
                taken = [
                    stage.at[h][pl.ds(k * local_j + j, local_a, stride=pitch), :]
                    for j in range(local_j)
                ]
                send_one[at * per_block + k, :, h * LANES : (h + 1) * LANES] = jnp.concatenate(
                    taken, axis=0
                ).astype(BF16)
            return inner

        lax.fori_loop(0, per_block, turn, 0)

        @pl.when(step == 0)
        def _():
            pl.semaphore_wait(barrier, size - 1 + groups - 1)

        def launch(k, inner):
            send_first(at * per_block + lax.rem(me + k, per_block), 0)
            return inner

        lax.fori_loop(0, per_block, launch, 0)
        return carry

    lax.fori_loop(0, blocks, first_block, 0)

    def launch_rest(k, carry):
        send_first(lax.rem(me + lax.rem(k, size), size), 1 + k // size)
        return carry

    lax.fori_loop(0, size * (CHUNKS - 1), launch_rest, 0)

    second_t[...] = second[...].T
    up_t[...] = up[...].T
    down_t[...] = down[...].T
    acc_up[...] = jnp.zeros_like(acc_up)
    acc_down[...] = jnp.zeros_like(acc_down)
    acc_second[...] = jnp.zeros_like(acc_second)
    acc_gain[...] = jnp.zeros_like(acc_gain)

    lane = lax.broadcasted_iota(jnp.int32, (rows, LANES), 1)

    def exchange(table, q, columns, send_sem, recv_sem):
        table[q, channel] = columns.T[:ROWS]
        for k in range(1, groups):
            pltpu.make_async_remote_copy(
                src_ref=table.at[q, channel],
                dst_ref=table.at[q, channel],
                send_sem=send_sem,
                recv_sem=recv_sem.at[q],
                device_id={"ch": lax.rem(channel + k, groups)},
                device_id_type=MESH,
            ).start()

    def collect(table, q, recv_sem):
        if groups > 1:
            others = table.at[q, : groups - 1]
            pltpu.make_async_copy(others, others, recv_sem.at[q]).wait()
        total = table[q, 0]
        for k in range(1, groups):
            total = total + table[q, k]
        return total / D

    def spread(values, wide):
        tall = jnp.concatenate([values] * (LANES // ROWS), axis=0).T
        for k in range(span):
            wide[k] = jnp.broadcast_to(tall[:, k : k + 1], (rows, LANES))

    def mix_chunk(q):
        part = pl.ds(pl.multiple_of(q * chunk_rows, chunk_rows), chunk_rows)
        arrived = recv_one.at[:, part]
        pltpu.make_async_copy(arrived, arrived, one_recv.at[q]).wait()
        columns = jnp.zeros((rows, LANES), F32)
        for pair in range(span // 2):
            at = pl.multiple_of(q * chunk_rows + pair * 2 * local_a, 2 * local_a)
            both = recv_one[:, pl.ds(at, 2 * local_a), :].astype(F32)
            for odd in range(2):
                k = 2 * pair + odd
                rows_k = both[:, odd * local_a : (odd + 1) * local_a, :]
                rows_k = rows_k.reshape(rows, width).astype(BF16)
                moved[q * span + k] = rows_k
                mixed = dot(second_t[...], rows_k)
                mixed_all[q * span + k] = mixed
                total = jnp.sum(mixed * mixed, axis=1, keepdims=True)
                columns = jnp.where(lane == k, total, columns)
        exchange(squares, q, columns, square_send, square_recv)

    def mlp_chunk(q):
        inverse = lax.rsqrt(collect(squares, q, square_recv) + EPSILON)
        inverse_rows[...] = inverse
        spread(inverse, inverse_wide)

        def tile(k, columns):
            j = q * span + k
            mixed = mixed_all[j]
            wide = jnp.concatenate([inverse_wide[k]] * halves, axis=1)
            scaled = mixed * wide
            gains = gain[...]
            normed = (scaled * gains).astype(BF16)
            upstream = cotangent[j]
            out = mixed
            grad_normed = jnp.zeros((rows, width), F32)
            for at in range(0, hidden, HIDDEN):
                part = slice(at, at + HIDDEN)
                pre = dot(normed, up[:, part])
                grad_act = dot(upstream, down_t[:, part])
                square = pre * pre
                curve = jnp.tanh(pre * (SLOPE + (SLOPE * CUBIC) * square))
                half = 0.5 + 0.5 * curve
                act = (pre * half).astype(BF16)
                bend = (1.0 - curve * curve) * pre
                slope = half + bend * (0.5 * SLOPE + (1.5 * SLOPE * CUBIC) * square)
                grad_pre = (grad_act * slope).astype(BF16)
                out = out + dot(act, down[part, :])
                grad_normed = grad_normed + dot(grad_pre, up_t[part, :])
                acc_down[:, part] += dot_rows(upstream, act)
                acc_up[:, part] += dot_rows(normed, grad_pre)
            layer_out[j] = out.astype(BF16)
            acc_gain[...] += jnp.sum(
                (grad_normed * scaled).reshape(rows // ROWS, ROWS, width), axis=0
            )
            grad_scaled = grad_normed * gains
            scaled_all[j] = grad_scaled
            total = jnp.sum(grad_scaled * mixed, axis=1, keepdims=True)
            return jnp.where(lane == k, total, columns)

        columns = lax.fori_loop(0, span, tile, jnp.zeros((rows, LANES), F32))
        exchange(crosses, q, columns, cross_send, cross_recv)

    def back_chunk(q):
        inverse = inverse_rows[...]
        spread(collect(crosses, q, cross_recv) * inverse * inverse * inverse, cross_wide)
        for pair in range(span // 2):
            turned = []
            for odd in range(2):
                k = 2 * pair + odd
                j = q * span + k
                wide = jnp.concatenate([inverse_wide[k]] * halves, axis=1)
                pull = jnp.concatenate([cross_wide[k]] * halves, axis=1)
                grad_mixed = (
                    cotangent[j].astype(F32) + wide * scaled_all[j] - pull * mixed_all[j]
                ).astype(BF16)
                acc_second[...] += dot_columns(moved[j], grad_mixed)
                turned.append(dot(second[...], grad_mixed).reshape(size, local_a, width))
            send_two[:, q * (span // 2) + pair] = jnp.concatenate(turned, axis=1).astype(BF16)

        pairs = pl.ds(q * (span // 2), span // 2)

        def launch(k, carry):
            target = lax.rem(me + k, size)
            pltpu.make_async_remote_copy(
                src_ref=send_two.at[target, pairs],
                dst_ref=recv_two.at[me, pairs],
                send_sem=two_send,
                recv_sem=two_recv.at[q],
                device_id={"ctx": target},
                device_id_type=MESH,
            ).start()
            return carry

        lax.fori_loop(1, size, launch, 0)
        pltpu.make_async_copy(
            send_two.at[me, pairs], recv_two.at[me, pairs], two_recv.at[q]
        ).start()

    mix_chunk(0)

    def chunk(q, carry):
        mlp_chunk(q)

        @pl.when(q < CHUNKS - 1)
        def _():
            mix_chunk(q + 1)

        back_chunk(q)
        return carry

    lax.fori_loop(0, CHUNKS, chunk, 0)

    def scatter(pack, got, index):
        def launch(k, carry):
            target = lax.rem(me + k, size)
            pltpu.make_async_remote_copy(
                src_ref=pack.at[target],
                dst_ref=got.at[me],
                send_sem=grad_send.at[index],
                recv_sem=grad_recv.at[index],
                device_id={"ctx": target},
                device_id_type=MESH,
            ).start()
            return carry

        lax.fori_loop(1, size, launch, 0)
        pltpu.make_async_copy(pack.at[me], got.at[me], grad_recv.at[index]).start()

    def gather(got, index):
        pltpu.make_async_copy(got, got, grad_recv.at[index]).wait()

        def add(k, total):
            return total + got[k].astype(F32)

        return lax.fori_loop(0, size, add, jnp.zeros(got.shape[1:], F32)) * grad_scale

    ups = lane_blocks(acc_up[...].reshape(size, width // size, hidden))
    seconds = lane_blocks(acc_second[...].reshape(size, local_a, rows))
    downs = lane_blocks(acc_down[...].T.reshape(size, hidden // size, width))
    gain_row = jnp.sum(acc_gain[...], axis=0, keepdims=True)
    gains = [
        jnp.broadcast_to(piece[None], (size, ROWS, LANES)) for piece in lane_blocks(gain_row)
    ]
    pieces = ups + seconds + downs + gains
    pieces = pieces + [gains[0]] * (len(pieces) % 2)
    at = 0
    while pieces:
        joined = pieces.pop(0)
        if joined.shape[1] % 16:
            joined = jnp.concatenate([joined, pieces.pop(0)], axis=1)
        pack_one[:, at : at + joined.shape[1], :] = joined.astype(BF16)
        at += joined.shape[1]
    scatter(pack_one, got_one, 0)

    pltpu.make_async_copy(recv_two, recv_two, two_recv.at[0]).wait() if CHUNKS == 1 else None
    if CHUNKS > 1:
        for q in range(CHUNKS):
            arrived = recv_two.at[:, q * (span // 2) : (q + 1) * (span // 2)]
            pltpu.make_async_copy(arrived, arrived, two_recv.at[q]).wait()

    def unpack(k, carry):
        value = recv_two[k].astype(F32).reshape(local_j * local_a, width)
        part = pl.ds(pl.multiple_of(k * local_j * local_a, local_j * local_a), local_j * local_a)
        for h, piece in enumerate(lane_blocks(value)):
            unpacked[h, part, :] = piece
        return carry

    lax.fori_loop(0, size, unpack, 0)
    acc_first[...] = jnp.zeros_like(acc_first)

    def back_row(a, carry):
        grad_gated = jnp.concatenate(
            [unpacked.at[h][pl.ds(a, positions, stride=local_a), :] for h in range(halves)], axis=1
        )
        inputs = signal[a]
        gate = lax.logistic(inputs.astype(F32))
        opened = grad_gated * gate
        grad_mix = opened.astype(BF16)
        grad_gate = opened * first_mix[a] * (1.0 - gate)
        grad_signal[a] = (dot(first[...], grad_mix) + grad_gate).astype(BF16)
        acc_first[...] += dot_columns(inputs, grad_mix)
        return carry

    lax.fori_loop(0, local_a, back_row, 0)
    pack_two[...] = acc_first[...].reshape(pack_two.shape).astype(BF16)
    scatter(pack_two, got_two, 1)

    total = gather(got_one, 0)
    at = 0
    for out in (out_up, out_second, out_down):
        height = out.shape[0]
        for h in range(out.shape[1] // LANES):
            out[:, h * LANES : (h + 1) * LANES] = total[at : at + height]
            at += height
    gain_sum = jnp.concatenate(
        [total[at + h * ROWS : at + (h + 1) * ROWS] for h in range(halves)], axis=1
    )
    turn = lax.rem(width - me * (width // size), width)
    out_gain[...] = pltpu.roll(gain_sum, turn, 1)[:, :LANES]
    out_first[...] = gather(got_two, 1)

    def drain(ref, sem):
        pltpu.make_async_copy(ref, ref, sem).wait()

    drain(send_one.at[: size - 1], one_send)
    drain(send_two.at[: size - 1], two_send)
    drain(pack_one.at[: size - 1], grad_send.at[0])
    drain(pack_two.at[: size - 1], grad_send.at[1])
    if groups > 1:
        drain(squares.at[:, : groups - 1], square_send)
        drain(crosses.at[:, : groups - 1], cross_send)


def shards(mesh, signal, factor_first, factor_second, up_weight, down_weight, norm_gain, cotangent):
    size, groups = mesh.shape["ctx"], mesh.shape["ch"]
    local_a, positions, width = signal.shape
    local_j, rows, _ = cotangent.shape
    hidden = up_weight.shape[2]
    halves = width // LANES
    span = local_j // CHUNKS
    block = min(128, positions)
    vmem = pl.BlockSpec(memory_space=pltpu.VMEM)
    packed = (
        width // size * (hidden // LANES)
        + local_a * (rows // LANES)
        + hidden // size * halves
        + ROWS * halves
    )
    packed += packed % 16

    def out(shape, dtype):
        return jax.ShapeDtypeStruct(shape, dtype)

    outs = (
        out(cotangent.shape, BF16),
        out(signal.shape, BF16),
        out((positions // size, positions), F32),
        out((rows // size, rows), F32),
        out((width // size, hidden), F32),
        out((hidden // size, width), F32),
        out((ROWS, LANES), F32),
    )
    dma = pltpu.SemaphoreType.DMA
    scratch = [
        pltpu.VMEM((positions, positions), BF16),
        pltpu.VMEM((rows, rows), BF16),
        pltpu.VMEM((hidden, width), BF16),
        pltpu.VMEM((width, hidden), BF16),
        pltpu.VMEM((local_a, positions, width), F32),
        pltpu.VMEM((halves, local_a * (block + ROWS), LANES), F32),
        pltpu.VMEM((size, local_j * local_a, width), BF16),
        pltpu.VMEM((size, local_j * local_a, width), BF16),
        pltpu.VMEM((local_j, rows, width), BF16),
        pltpu.VMEM((local_j, rows, width), F32),
        pltpu.VMEM((local_j, rows, width), F32),
        pltpu.VMEM((CHUNKS, groups, ROWS, rows), F32),
        pltpu.VMEM((CHUNKS, groups, ROWS, rows), F32),
        pltpu.VMEM((ROWS, rows), F32),
        pltpu.VMEM((span, rows, LANES), F32),
        pltpu.VMEM((span, rows, LANES), F32),
        pltpu.VMEM((size, local_j // 2, 2 * local_a, width), BF16),
        pltpu.VMEM((size, local_j // 2, 2 * local_a, width), BF16),
        pltpu.VMEM((halves, positions * local_a, LANES), F32),
        pltpu.VMEM((width, hidden), F32),
        pltpu.VMEM((width, hidden), F32),
        pltpu.VMEM((rows, rows), F32),
        pltpu.VMEM((positions, positions), F32),
        pltpu.VMEM((ROWS, width), F32),
        pltpu.VMEM((size, packed, LANES), BF16),
        pltpu.VMEM((size, packed, LANES), BF16),
        pltpu.VMEM((size, positions // size, positions), BF16),
        pltpu.VMEM((size, positions // size, positions), BF16),
        dma, dma((CHUNKS,)), dma, dma((CHUNKS,)), dma, dma((CHUNKS,)), dma, dma((CHUNKS,)),
        dma((2,)), dma((2,)),
    ]
    results = pl.pallas_call(
        functools.partial(kernel, groups),
        out_shape=outs,
        in_specs=[vmem] * 7,
        out_specs=(vmem,) * 7,
        scratch_shapes=scratch,
        compiler_params=pltpu.CompilerParams(
            collective_id=0, has_side_effects=True, vmem_limit_bytes=67043328
        ),
    )(signal, factor_first[0], factor_second[0], up_weight[0], down_weight[0], norm_gain, cotangent)
    gain = results[6][:1, : width // size]
    return results[:2] + tuple(value[None] for value in results[2:6]) + (gain,)


def solution(mesh):
    placed = (
        P("ctx", None, "ch"),
        P("ch", None, None),
        P("ch", None, None),
        P("ch", None, None),
        P("ch", None, None),
        P("ch", None),
        P("ctx", None, "ch"),
    )
    return jax.shard_map(
        functools.partial(shards, mesh),
        mesh=mesh,
        in_specs=placed,
        out_specs=(
            P("ctx", None, "ch"),
            P("ctx", None, "ch"),
            P("ch", "ctx", None),
            P("ch", "ctx", None),
            P("ch", "ctx", None),
            P("ch", "ctx", None),
            P("ch", "ctx"),
        ),
        check_vma=False,
    )
```

```python
import functools
import math

import jax
import jax.numpy as jnp
from jax import lax
from jax.experimental import pallas as pl
from jax.experimental.pallas import tpu as pltpu
from jax.sharding import PartitionSpec as P

D = 1024
EPSILON = 1e-05
CHUNKS = 4
LANES = 128
ROWS = 8
HIDDEN = 256
PAIR = 2
MESH = pl.DeviceIdType.MESH
BF16 = jnp.bfloat16
F32 = jnp.float32
CUBIC = 0.044715
SLOPE = math.sqrt(2.0 / math.pi)


def dot(lhs, rhs):
    return jnp.dot(lhs, rhs, preferred_element_type=F32)


def dot_rows(lhs, rhs):
    return lax.dot_general(lhs, rhs, (((0,), (0,)), ((), ())), preferred_element_type=F32)


def dot_columns(lhs, rhs):
    return lax.dot_general(lhs, rhs, (((1,), (1,)), ((), ())), preferred_element_type=F32)


def lane_blocks(value):
    return [value[..., at : at + LANES] for at in range(0, value.shape[-1], LANES)]


OUT = pltpu.VMEM
LIMIT = 61865984

def kernel(
    groups, signal_in, first_in, second_in, up_in, down_in, gain_in, cotangent_in,
    layer_out, grad_signal, out_first, out_second, out_up, out_down, out_gain,
    signal, first, second, up, down, gain, cotangent,
    first_t, second_t, up_t, down_t, first_mix, stage, send_one, recv_one, moved, mixed_all,
    scaled_all, grad_acts, squares, crosses, inverse_rows, inverse_wide, cross_wide, send_two,
    recv_two, unpacked, acc_up, acc_down, acc_second, acc_first, acc_gain, pack_up, got_up,
    pack_rest, got_rest, pack_first, got_first, load_sem, one_send, one_recv, two_send, two_recv,
    square_send, square_recv, cross_send, cross_recv, grad_send, grad_recv,
):
    me = lax.axis_index("ctx")
    channel = lax.axis_index("ch")
    local_a, positions, width = signal.shape
    local_j, rows, _ = cotangent.shape
    hidden = up.shape[1]
    size = rows // local_a
    span = local_j // CHUNKS
    block = stage.shape[1] // local_a - ROWS
    per_block = block // local_j
    blocks = positions // block
    pitch = block + ROWS
    chunk_rows = span * local_a
    halves = width // LANES
    grad_scale = 1.0 / math.sqrt(rows * positions)

    loads = [
        pltpu.make_async_copy(source, target, load_sem.at[k])
        for k, (source, target) in enumerate(
            zip(
                (first_in, signal_in, second_in, up_in, down_in, gain_in, cotangent_in),
                (first, signal, second, up, down, gain, cotangent),
            )
        )
    ]
    for load in loads:
        load.start()

    barrier = pltpu.get_barrier_semaphore()

    def greet(k, carry):
        pl.semaphore_signal(
            barrier, inc=1, device_id={"ctx": lax.rem(me + k, size)}, device_id_type=MESH
        )
        return carry

    lax.fori_loop(1, size, greet, 0)
    for k in range(1, groups):
        pl.semaphore_signal(
            barrier, inc=1, device_id={"ch": lax.rem(channel + k, groups)}, device_id_type=MESH
        )

    loads[0].wait()
    first_t[...] = first[...].T
    loads[1].wait()

    def first_block(at, carry):
        part = pl.ds(pl.multiple_of(at * block, block), block)
        weights = first_t[part, :]
        for a in range(local_a):
            mix = dot(weights, signal[a])
            first_mix[a, part, :] = mix
            gated = mix * lax.logistic(signal[a, part, :].astype(F32))
            for h, piece in enumerate(lane_blocks(gated)):
                stage[h, a * pitch : a * pitch + block, :] = piece

        def turn(k, inner):
            for h in range(halves):
                taken = [
                    stage.at[h][pl.ds(k * local_j + j, local_a, stride=pitch), :]
                    for j in range(local_j)
                ]
                send_one[at * per_block + k, :, h * LANES : (h + 1) * LANES] = jnp.concatenate(
                    taken, axis=0
                ).astype(BF16)
            return inner

        lax.fori_loop(0, per_block, turn, 0)
        return carry

    lax.fori_loop(0, blocks, first_block, 0)
    pl.semaphore_wait(barrier, size - 1 + groups - 1)

    half = size // 4

    def send_part(source, target, part, send_sem, recv_sem, odd, start, stop):
        def launch(k, carry):
            peer = lax.rem(me + 2 * k + odd, size)
            pltpu.make_async_remote_copy(
                src_ref=source.at[peer, part],
                dst_ref=target.at[me, part],
                send_sem=send_sem,
                recv_sem=recv_sem,
                device_id={"ctx": peer},
                device_id_type=MESH,
            ).start()
            return carry

        lax.fori_loop(start, stop, launch, 0)

    def send_near(source, target, part, send_sem, recv_sem):
        send_part(source, target, part, send_sem, recv_sem, 0, 1, 2 * half)
        pltpu.make_async_copy(source.at[me, part], target.at[me, part], recv_sem).start()

    def send_far(*route, start=0, stop=2):
        send_part(*route, 1, start * half, stop * half)

    def first_route(q):
        part = pl.ds(pl.multiple_of(q * chunk_rows, chunk_rows), chunk_rows)
        return send_one, recv_one, part, one_send, one_recv.at[q]

    def second_route(q):
        part = pl.ds(q * (span // 2), span // 2)
        return send_two, recv_two, part, two_send, two_recv.at[q]

    def grad_route(pack, got, index):
        part = pl.ds(0, pack.shape[1])
        return pack, got, part, grad_send.at[index], grad_recv.at[index]

    send_far(*first_route(0))
    send_near(*first_route(0))
    send_far(*first_route(1), stop=1)
    send_near(*first_route(1))
    for load in loads[2:]:
        load.wait()
    second_t[...] = second[...].T
    up_t[...] = up[...].T
    down[...] = (down[...].astype(F32) * 0.5).astype(BF16)
    down_t[...] = down[...].T
    acc_up[...] = jnp.zeros_like(acc_up)
    acc_down[...] = jnp.zeros_like(acc_down)
    acc_second[...] = jnp.zeros_like(acc_second)
    acc_first[...] = jnp.zeros_like(acc_first)
    acc_gain[...] = jnp.zeros_like(acc_gain)

    def grad_act_rows(j, carry):
        grad_acts[j] = dot(cotangent[j], down_t[...]).astype(BF16)
        return carry

    lax.fori_loop(0, local_j * 3 // 4, grad_act_rows, 0)

    lane = lax.broadcasted_iota(jnp.int32, (rows, LANES), 1)

    def exchange(table, q, columns, send_sem, recv_sem):
        table[q, channel] = columns.T[:ROWS]
        for k in range(1, groups):
            pltpu.make_async_remote_copy(
                src_ref=table.at[q, channel],
                dst_ref=table.at[q, channel],
                send_sem=send_sem,
                recv_sem=recv_sem.at[q],
                device_id={"ch": lax.rem(channel + k, groups)},
                device_id_type=MESH,
            ).start()

    def collect(table, q, recv_sem):
        if groups > 1:
            others = table.at[q, : groups - 1]
            pltpu.make_async_copy(others, others, recv_sem.at[q]).wait()
        total = table[q, 0]
        for k in range(1, groups):
            total = total + table[q, k]
        return total / D

    def spread(values, wide, at):
        tall = jnp.concatenate([values] * (LANES // ROWS), axis=0).T
        for k in range(span):
            wide[at + k] = jnp.broadcast_to(tall[:, k : k + 1], (rows, LANES))

    def mix_chunk(q):
        part = pl.ds(pl.multiple_of(q * chunk_rows, chunk_rows), chunk_rows)
        arrived = recv_one.at[:, part]
        pltpu.make_async_copy(arrived, arrived, one_recv.at[q]).wait()
        columns = jnp.zeros((rows, LANES), F32)
        for pair in range(span // 2):
            at = pl.multiple_of(q * chunk_rows + pair * 2 * local_a, 2 * local_a)
            both = recv_one[:, pl.ds(at, 2 * local_a), :].astype(F32)
            for odd in range(2):
                k = 2 * pair + odd
                rows_k = both[:, odd * local_a : (odd + 1) * local_a, :]
                rows_k = rows_k.reshape(rows, width).astype(BF16)
                moved[q * span + k] = rows_k
                mixed = dot(second_t[...], rows_k)
                mixed_all[q * span + k] = mixed
                total = jnp.sum(mixed * mixed, axis=1, keepdims=True)
                columns = jnp.where(lane == k, total, columns)
        exchange(squares, q, columns, square_send, square_recv)

    def mlp_tile(q, step):
        j = q * span + step * PAIR
        slot = lax.rem(q, 2) * span + step * PAIR
        count = PAIR * rows
        mixed = mixed_all[pl.ds(j, PAIR)].reshape(count, width)
        wide = inverse_wide[pl.ds(slot, PAIR)].reshape(count, LANES)
        scaled = mixed * jnp.concatenate([wide] * halves, axis=1)
        gains = gain[...]
        normed = (scaled * gains).astype(BF16)
        upstream = cotangent[pl.ds(j, PAIR)].reshape(count, width)
        out = mixed
        grad_normed = None
        parts = [slice(at, at + HIDDEN) for at in range(0, hidden, HIDDEN)]
        ready = dot(normed, up[:, parts[0]])
        for n, part in enumerate(parts):
            pre = ready
            if n + 1 < len(parts):
                ready = dot(normed, up[:, parts[n + 1]])
            grad_act = grad_acts[pl.ds(j, PAIR), :, part].reshape(count, HIDDEN).astype(F32)
            base = SLOPE + (SLOPE * CUBIC) * (pre * pre)
            curve = jnp.tanh(pre * base)
            opened = 1.0 + curve
            act = (pre * opened).astype(BF16)
            bend = pre * (3.0 * base - 2.0 * SLOPE)
            grad_pre = (grad_act * (opened * (1.0 + (1.0 - curve) * bend))).astype(BF16)
            out = out + dot(act, down[part, :])
            back = dot(grad_pre, up_t[part, :])
            grad_normed = back if grad_normed is None else grad_normed + back
            acc_down[:, part] += dot_rows(upstream, act)
            acc_up[:, part] += dot_rows(normed, grad_pre)
        layer_out[pl.ds(j, PAIR)] = out.astype(BF16).reshape(PAIR, rows, width)
        acc_gain[...] += jnp.sum(
            (grad_normed * scaled).reshape(count // ROWS, ROWS, width), axis=0
        )
        grad_scaled = grad_normed * gains
        scaled_all[pl.ds(j, PAIR)] = grad_scaled.reshape(PAIR, rows, width)
        total = jnp.sum(grad_scaled * mixed, axis=1, keepdims=True)
        cross_wide[pl.ds(slot, PAIR)] = jnp.broadcast_to(total, (count, LANES)).reshape(
            PAIR, rows, LANES
        )

    def send_cross(q):
        at = lax.rem(q, 2) * span
        columns = jnp.zeros((rows, LANES), F32)
        for k in range(span):
            columns = jnp.where(lane == k, cross_wide[at + k], columns)
        exchange(crosses, q, columns, cross_send, cross_recv)

    def back_chunk(q):
        at = lax.rem(q, 2) * span
        inverse = inverse_rows[lax.rem(q, 2)]
        spread(collect(crosses, q, cross_recv) * inverse * inverse * inverse, cross_wide, at)
        for pair in range(span // 2):
            turned = []
            for odd in range(2):
                k = 2 * pair + odd
                j = q * span + k
                wide = jnp.concatenate([inverse_wide[at + k]] * halves, axis=1)
                pull = jnp.concatenate([cross_wide[at + k]] * halves, axis=1)
                grad_mixed = (
                    cotangent[j].astype(F32) + wide * scaled_all[j] - pull * mixed_all[j]
                ).astype(BF16)
                acc_second[...] += dot_columns(moved[j], grad_mixed)
                turned.append(dot(second[...], grad_mixed).reshape(size, local_a, width))
            send_two[:, q * (span // 2) + pair] = jnp.concatenate(turned, axis=1).astype(BF16)

    mix_chunk(0)
    send_far(*first_route(1), start=1)
    send_far(*first_route(2), stop=1)
    send_near(*first_route(2))
    lax.fori_loop(local_j * 3 // 4, local_j, grad_act_rows, 0)

    def chunk(q, carry):
        inverse = lax.rsqrt(collect(squares, q, square_recv) + EPSILON)
        inverse_rows[lax.rem(q, 2)] = inverse
        spread(inverse, inverse_wide, lax.rem(q, 2) * span)

        def tile(step, inner):
            mlp_tile(q, step)

            @pl.when((step == 0) & (q < CHUNKS - 1))
            def _():
                mix_chunk(q + 1)

            @pl.when((step == 0) & (q < CHUNKS - 2))
            def _():
                send_far(*first_route(q + 2), start=1)

            @pl.when((step == 0) & (q < CHUNKS - 3))
            def _():
                send_far(*first_route(q + 3), stop=1)
                send_near(*first_route(q + 3))

            @pl.when((step == 0) & (q > 0))
            def _():
                back_chunk(q - 1)
                send_near(*second_route(q - 1))

            return inner

        lax.fori_loop(0, span // PAIR, tile, 0)
        send_cross(q)

        @pl.when(q > 0)
        def _():
            send_far(*second_route(q - 1))

        return carry

    lax.fori_loop(0, CHUNKS, chunk, 0)

    def pack(target, pieces):
        at = 0
        while pieces:
            joined = pieces.pop(0)
            if joined.shape[1] % 16:
                joined = jnp.concatenate([joined, pieces.pop(0)], axis=1)
            target[:, at : at + joined.shape[1], :] = joined.astype(BF16)
            at += joined.shape[1]

    pack(pack_up, lane_blocks(acc_up[...].reshape(size, width // size, hidden)))
    send_near(*grad_route(pack_up, got_up, 0))
    back_chunk(CHUNKS - 1)
    send_far(*second_route(CHUNKS - 1))
    send_near(*second_route(CHUNKS - 1))
    send_far(*grad_route(pack_up, got_up, 0))

    seconds = lane_blocks(acc_second[...].reshape(size, local_a, rows))
    downs = lane_blocks((acc_down[...] * 0.5).T.reshape(size, hidden // size, width))
    gain_row = jnp.sum(acc_gain[...], axis=0, keepdims=True)
    gains = [
        jnp.broadcast_to(piece[None], (size, ROWS, LANES)) for piece in lane_blocks(gain_row)
    ]
    pack(pack_rest, seconds + downs + gains)
    send_far(*grad_route(pack_rest, got_rest, 1))
    send_near(*grad_route(pack_rest, got_rest, 1))

    chunk_height = span * local_a
    for q in range(CHUNKS):
        arrived = recv_two.at[:, q * (span // 2) : (q + 1) * (span // 2)]
        pltpu.make_async_copy(arrived, arrived, two_recv.at[q]).wait()

        def unpack(k, carry):
            value = recv_two[k, q * (span // 2) : (q + 1) * (span // 2)].astype(F32)
            value = value.reshape(chunk_height, width)
            at = pl.multiple_of(k * local_j * local_a + q * chunk_height, chunk_height)
            for h, piece in enumerate(lane_blocks(value)):
                unpacked[h, pl.ds(at, chunk_height), :] = piece
            return carry

        lax.fori_loop(0, size, unpack, 0, unroll=4)

    def back_row(step, carry):
        for odd in range(2):
            a = step * 2 + odd
            grad_gated = jnp.concatenate(
                [
                    unpacked.at[h][pl.ds(a, positions, stride=local_a), :]
                    for h in range(halves)
                ],
                axis=1,
            )
            inputs = signal[a]
            gate = lax.logistic(inputs.astype(F32))
            opened = grad_gated * gate
            grad_mix = opened.astype(BF16)
            grad_gate = opened * first_mix[a] * (1.0 - gate)
            grad_signal[a] = (dot(first[...], grad_mix) + grad_gate).astype(BF16)
            acc_first[...] += dot_columns(inputs, grad_mix)
        return carry

    lax.fori_loop(0, local_a // 2, back_row, 0)
    pack_first[...] = acc_first[...].reshape(pack_first.shape).astype(BF16)
    send_far(*grad_route(pack_first, got_first, 2))
    send_near(*grad_route(pack_first, got_first, 2))

    def gather(got, index):
        pltpu.make_async_copy(got, got, grad_recv.at[index]).wait()

        def add(k, total):
            return total + got[k].astype(F32)

        zero = jnp.zeros(got.shape[1:], F32)
        return lax.fori_loop(0, size, add, zero, unroll=4) * grad_scale

    def unfold(out, total, at):
        height = out.shape[0]
        for h in range(out.shape[1] // LANES):
            out[:, h * LANES : (h + 1) * LANES] = total[at : at + height]
            at += height
        return at

    unfold(out_up, gather(got_up, 0), 0)
    total = gather(got_rest, 1)
    at = unfold(out_second, total, 0)
    at = unfold(out_down, total, at)
    gain_sum = jnp.concatenate(
        [total[at + h * ROWS : at + (h + 1) * ROWS] for h in range(halves)], axis=1
    )
    turn = lax.rem(width - me * (width // size), width)
    out_gain[...] = pltpu.roll(gain_sum, turn, 1)[:, :LANES]
    out_first[...] = gather(got_first, 2)

    def drain(ref, sem):
        pltpu.make_async_copy(ref, ref, sem).wait()

    drain(send_one.at[: size - 1], one_send)
    drain(send_two.at[: size - 1], two_send)
    drain(pack_up.at[: size - 1], grad_send.at[0])
    drain(pack_rest.at[: size - 1], grad_send.at[1])
    drain(pack_first.at[: size - 1], grad_send.at[2])
    if groups > 1:
        drain(squares.at[:, : groups - 1], square_send)
        drain(crosses.at[:, : groups - 1], cross_send)


def finish(*refs):
    sources, targets, sems = refs[:7], refs[7:14], refs[14]
    copies = [
        pltpu.make_async_copy(sources[k], targets[k], sems.at[k]) for k in range(6)
    ]
    for copy in copies:
        copy.start()
    targets[6][...] = sources[6][:1, : targets[6].shape[1]]
    for copy in copies:
        copy.wait()


def shards(mesh, signal, factor_first, factor_second, up_weight, down_weight, norm_gain, cotangent):
    size, groups = mesh.shape["ctx"], mesh.shape["ch"]
    local_a, positions, width = signal.shape
    local_j, rows, _ = cotangent.shape
    hidden = up_weight.shape[2]
    halves = width // LANES
    span = local_j // CHUNKS
    block = min(128, positions)
    vmem = pl.BlockSpec(memory_space=pltpu.VMEM)
    anywhere = pl.BlockSpec(memory_space=pl.ANY)
    up_rows = width // size * (hidden // LANES)
    rest_rows = local_a * (rows // LANES) + hidden // size * halves + ROWS * halves

    results = (
        (cotangent.shape, BF16),
        (signal.shape, BF16),
        ((positions // size, positions), F32),
        ((rows // size, rows), F32),
        ((width // size, hidden), F32),
        ((hidden // size, width), F32),
    )
    dma = pltpu.SemaphoreType.DMA
    scratch = [
        pltpu.VMEM(signal.shape, BF16),
        pltpu.VMEM((positions, positions), BF16),
        pltpu.VMEM((rows, rows), BF16),
        pltpu.VMEM((width, hidden), BF16),
        pltpu.VMEM((hidden, width), BF16),
        pltpu.VMEM((1, width), F32),
        pltpu.VMEM(cotangent.shape, BF16),
        pltpu.VMEM((positions, positions), BF16),
        pltpu.VMEM((rows, rows), BF16),
        pltpu.VMEM((hidden, width), BF16),
        pltpu.VMEM((width, hidden), BF16),
        pltpu.VMEM((local_a, positions, width), F32),
        pltpu.VMEM((halves, local_a * (block + ROWS), LANES), F32),
        pltpu.VMEM((size, local_j * local_a, width), BF16),
        pltpu.VMEM((size, local_j * local_a, width), BF16),
        pltpu.VMEM((local_j, rows, width), BF16),
        pltpu.VMEM((local_j, rows, width), F32),
        pltpu.VMEM((local_j, rows, width), F32),
        pltpu.VMEM((local_j, rows, hidden), BF16),
        pltpu.VMEM((CHUNKS, groups, ROWS, rows), F32),
        pltpu.VMEM((CHUNKS, groups, ROWS, rows), F32),
        pltpu.VMEM((2, ROWS, rows), F32),
        pltpu.VMEM((2 * span, rows, LANES), F32),
        pltpu.VMEM((2 * span, rows, LANES), F32),
        pltpu.VMEM((size, local_j // 2, 2 * local_a, width), BF16),
        pltpu.VMEM((size, local_j // 2, 2 * local_a, width), BF16),
        pltpu.VMEM((halves, positions * local_a, LANES), F32),
        pltpu.VMEM((width, hidden), F32),
        pltpu.VMEM((width, hidden), F32),
        pltpu.VMEM((rows, rows), F32),
        pltpu.VMEM((positions, positions), F32),
        pltpu.VMEM((ROWS, width), F32),
        pltpu.VMEM((size, up_rows, LANES), BF16),
        pltpu.VMEM((size, up_rows, LANES), BF16),
        pltpu.VMEM((size, rest_rows, LANES), BF16),
        pltpu.VMEM((size, rest_rows, LANES), BF16),
        pltpu.VMEM((size, positions // size, positions), BF16),
        pltpu.VMEM((size, positions // size, positions), BF16),
        dma((7,)), dma, dma((CHUNKS,)), dma, dma((CHUNKS,)), dma, dma((CHUNKS,)), dma,
        dma((CHUNKS,)), dma((3,)), dma((3,)),
    ]
    values = pl.pallas_call(
        functools.partial(kernel, groups),
        out_shape=tuple(OUT(*result) for result in results) + (OUT((ROWS, LANES), F32),),
        in_specs=[anywhere] * 7,
        out_specs=(vmem,) * 7,
        scratch_shapes=scratch,
        compiler_params=pltpu.CompilerParams(
            collective_id=0, has_side_effects=True, vmem_limit_bytes=LIMIT
        ),
    )(signal, factor_first[0], factor_second[0], up_weight[0], down_weight[0], norm_gain, cotangent)
    shapes = [jax.ShapeDtypeStruct(*result) for result in results]
    values = pl.pallas_call(
        finish,
        out_shape=(*shapes, jax.ShapeDtypeStruct((1, width // size), F32)),
        in_specs=[vmem] * 7,
        out_specs=(anywhere,) * 6 + (vmem,),
        scratch_shapes=[dma((6,))],
        compiler_params=pltpu.CompilerParams(vmem_limit_bytes=4194304),
    )(*[pltpu.with_memory_space_constraint(value, pltpu.VMEM) for value in values])
    return (*values[:2], *(value[None] for value in values[2:6]), values[6])


def solution(mesh):
    placed = (
        P("ctx", None, "ch"),
        P("ch", None, None),
        P("ch", None, None),
        P("ch", None, None),
        P("ch", None, None),
        P("ch", None),
        P("ctx", None, "ch"),
    )
    return jax.shard_map(
        functools.partial(shards, mesh),
        mesh=mesh,
        in_specs=placed,
        out_specs=(
            P("ctx", None, "ch"),
            P("ctx", None, "ch"),
            P("ch", "ctx", None),
            P("ch", "ctx", None),
            P("ch", "ctx", None),
            P("ch", "ctx", None),
            P("ch", "ctx"),
        ),
        check_vma=False,
    )
```

```python
import functools
import math

import jax
import jax.numpy as jnp
from jax import lax
from jax.experimental import pallas as pl
from jax.experimental.pallas import tpu as pltpu
from jax.sharding import PartitionSpec as P

D = 1024
EPSILON = 1e-05
CHUNKS = 4
LANES = 128
ROWS = 8
HIDDEN = 256
PAIR = 2
STRIDE = 5
MESH = pl.DeviceIdType.MESH
BF16 = jnp.bfloat16
F32 = jnp.float32
CUBIC = 0.044715
SLOPE = math.sqrt(2.0 / math.pi)


def dot(lhs, rhs):
    return jnp.dot(lhs, rhs, preferred_element_type=F32)


def dot_rows(lhs, rhs):
    return lax.dot_general(lhs, rhs, (((0,), (0,)), ((), ())), preferred_element_type=F32)


def dot_columns(lhs, rhs):
    return lax.dot_general(lhs, rhs, (((1,), (1,)), ((), ())), preferred_element_type=F32)


def lane_blocks(value):
    return [value[..., at : at + LANES] for at in range(0, value.shape[-1], LANES)]


OUT = pltpu.VMEM
LIMIT = 61865984

def kernel(
    groups, signal_in, first_in, second_in, up_in, down_in, gain_in, cotangent_in,
    layer_out, grad_signal, out_first, out_second, out_up, out_down, out_gain,
    signal, first, second, up, down, gain, cotangent,
    first_t, second_t, up_t, down_t, first_mix, stage, send_one, recv_one, moved, mixed_all,
    scaled_all, grad_acts, squares, crosses, inverse_rows, inverse_wide, cross_wide, send_two,
    recv_two, unpacked, acc_up, acc_down, acc_second, acc_first, acc_gain, grad_mixes, pack_up,
    got_far, pack_near, got_up, pack_rest, got_rest, pack_last, got_last, pack_first, got_first, load_sem, one_send, one_recv, two_send, two_recv,
    square_send, square_recv, cross_send, cross_recv, grad_send, grad_recv,
):
    me = lax.axis_index("ctx")
    channel = lax.axis_index("ch")
    local_a, positions, width = signal.shape
    local_j, rows, _ = cotangent.shape
    hidden = up.shape[1]
    size = rows // local_a
    span = local_j // CHUNKS
    block = stage.shape[1] // local_a - ROWS
    per_block = block // local_j
    blocks = positions // block
    pitch = block + ROWS
    chunk_rows = span * local_a
    halves = width // LANES
    grad_scale = 1.0 / math.sqrt(rows * positions)

    loads = [
        pltpu.make_async_copy(source, target, load_sem.at[k])
        for k, (source, target) in enumerate(
            zip(
                (first_in, signal_in, second_in, up_in, down_in, gain_in, cotangent_in),
                (first, signal, second, up, down, gain, cotangent),
            )
        )
    ]
    for load in loads:
        load.start()

    barrier = pltpu.get_barrier_semaphore()

    def greet(k, carry):
        pl.semaphore_signal(
            barrier, inc=1, device_id={"ctx": lax.rem(me + k, size)}, device_id_type=MESH
        )
        return carry

    lax.fori_loop(1, size, greet, 0)
    for k in range(1, groups):
        pl.semaphore_signal(
            barrier, inc=1, device_id={"ch": lax.rem(channel + k, groups)}, device_id_type=MESH
        )

    loads[0].wait()
    first_t[...] = first[...].T
    loads[1].wait()

    def first_block(at, carry):
        part = pl.ds(pl.multiple_of(at * block, block), block)
        weights = first_t[part, :]
        for a in range(local_a):
            mix = dot(weights, signal[a])
            first_mix[a, part, :] = mix
            gated = mix * lax.logistic(signal[a, part, :].astype(F32))
            for h, piece in enumerate(lane_blocks(gated)):
                stage[h, a * pitch : a * pitch + block, :] = piece

        def turn(k, inner):
            for h in range(halves):
                taken = [
                    stage.at[h][pl.ds(k * local_j + j, local_a, stride=pitch), :]
                    for j in range(local_j)
                ]
                send_one[at * per_block + k, :, h * LANES : (h + 1) * LANES] = jnp.concatenate(
                    taken, axis=0
                ).astype(BF16)
            return inner

        lax.fori_loop(0, per_block, turn, 0)
        return carry

    lax.fori_loop(0, blocks, first_block, 0)
    pl.semaphore_wait(barrier, size - 1 + groups - 1)

    half = size // 4

    def send_part(source, target, part, send_sem, recv_sem, odd, start, stop):
        def launch(k, carry):
            peer = lax.rem(me + 2 * lax.rem(STRIDE * k, size // 2) + odd, size)
            pltpu.make_async_remote_copy(
                src_ref=source.at[peer, part],
                dst_ref=target.at[me, part],
                send_sem=send_sem,
                recv_sem=recv_sem,
                device_id={"ctx": peer},
                device_id_type=MESH,
            ).start()
            return carry

        lax.fori_loop(start, stop, launch, 0)

    def send_near(source, target, part, send_sem, recv_sem):
        send_part(source, target, part, send_sem, recv_sem, 0, 1, 2 * half)
        pltpu.make_async_copy(source.at[me, part], target.at[me, part], recv_sem).start()

    def send_far(*route, start=0, stop=2):
        send_part(*route, 1, start * half, stop * half)

    def first_route(q):
        part = pl.ds(pl.multiple_of(q * chunk_rows, chunk_rows), chunk_rows)
        return send_one, recv_one, part, one_send, one_recv.at[q]

    def second_route(q):
        part = pl.ds(q * (span // 2), span // 2)
        return send_two, recv_two, part, two_send, two_recv.at[q]

    send_far(*first_route(0))
    send_near(*first_route(0))
    send_far(*first_route(1), stop=1)
    send_near(*first_route(1))
    for load in loads[2:]:
        load.wait()
    second_t[...] = second[...].T
    up_t[...] = up[...].T
    down[...] = (down[...].astype(F32) * 0.5).astype(BF16)
    down_t[...] = down[...].T
    acc_up[...] = jnp.zeros_like(acc_up)
    acc_down[...] = jnp.zeros_like(acc_down)
    acc_second[...] = jnp.zeros_like(acc_second)
    acc_first[...] = jnp.zeros_like(acc_first)
    acc_gain[...] = jnp.zeros_like(acc_gain)

    def grad_act_rows(j, carry):
        grad_acts[j] = dot(cotangent[j], down_t[...]).astype(BF16)
        return carry

    lax.fori_loop(0, local_j * 3 // 4, grad_act_rows, 0)

    lane = lax.broadcasted_iota(jnp.int32, (rows, LANES), 1)

    def exchange(table, q, columns, send_sem, recv_sem):
        table[q, channel] = columns.T[:ROWS]
        for k in range(1, groups):
            pltpu.make_async_remote_copy(
                src_ref=table.at[q, channel],
                dst_ref=table.at[q, channel],
                send_sem=send_sem,
                recv_sem=recv_sem.at[q],
                device_id={"ch": lax.rem(channel + k, groups)},
                device_id_type=MESH,
            ).start()

    def collect(table, q, recv_sem):
        if groups > 1:
            others = table.at[q, : groups - 1]
            pltpu.make_async_copy(others, others, recv_sem.at[q]).wait()
        total = table[q, 0]
        for k in range(1, groups):
            total = total + table[q, k]
        return total / D

    def spread(values, wide, at):
        tall = jnp.concatenate([values] * (LANES // ROWS), axis=0).T
        for k in range(span):
            wide[at + k] = jnp.broadcast_to(tall[:, k : k + 1], (rows, LANES))

    def mix_chunk(q):
        part = pl.ds(pl.multiple_of(q * chunk_rows, chunk_rows), chunk_rows)
        arrived = recv_one.at[:, part]
        pltpu.make_async_copy(arrived, arrived, one_recv.at[q]).wait()
        columns = jnp.zeros((rows, LANES), F32)
        for pair in range(span // 2):
            at = pl.multiple_of(q * chunk_rows + pair * 2 * local_a, 2 * local_a)
            both = recv_one[:, pl.ds(at, 2 * local_a), :].astype(F32)
            for odd in range(2):
                k = 2 * pair + odd
                rows_k = both[:, odd * local_a : (odd + 1) * local_a, :]
                rows_k = rows_k.reshape(rows, width).astype(BF16)
                moved[q * span + k] = rows_k
                mixed = dot(second_t[...], rows_k)
                mixed_all[q * span + k] = mixed
                total = jnp.sum(mixed * mixed, axis=1, keepdims=True)
                columns = jnp.where(lane == k, total, columns)
        exchange(squares, q, columns, square_send, square_recv)

    def mlp_tile(q, step):
        j = q * span + step * PAIR
        slot = lax.rem(q, 2) * span + step * PAIR
        count = PAIR * rows
        mixed = mixed_all[pl.ds(j, PAIR)].reshape(count, width)
        wide = inverse_wide[pl.ds(slot, PAIR)].reshape(count, LANES)
        scaled = mixed * jnp.concatenate([wide] * halves, axis=1)
        gains = gain[...]
        normed = (scaled * gains).astype(BF16)
        upstream = cotangent[pl.ds(j, PAIR)].reshape(count, width)
        out = mixed
        grad_normed = None
        parts = [slice(at, at + HIDDEN) for at in range(0, hidden, HIDDEN)]
        queue = [dot(normed, up[:, parts[0]]), dot(normed, up[:, parts[1]])]
        for n, part in enumerate(parts):
            pre = queue.pop(0)
            if n + 2 < len(parts):
                queue.append(dot(normed, up[:, parts[n + 2]]))
            grad_act = grad_acts[pl.ds(j, PAIR), :, part].reshape(count, HIDDEN).astype(F32)
            base = SLOPE + (SLOPE * CUBIC) * (pre * pre)
            curve = jnp.tanh(pre * base)
            opened = 1.0 + curve
            act = (pre * opened).astype(BF16)
            bend = pre * (3.0 * base - 2.0 * SLOPE)
            grad_pre = (grad_act * (opened * (1.0 + (1.0 - curve) * bend))).astype(BF16)
            out = out + dot(act, down[part, :])
            back = dot(grad_pre, up_t[part, :])
            grad_normed = back if grad_normed is None else grad_normed + back
            acc_down[:, part] += dot_rows(upstream, act)
            acc_up[:, part] += dot_rows(normed, grad_pre)
        layer_out[pl.ds(j, PAIR)] = out.astype(BF16).reshape(PAIR, rows, width)
        acc_gain[...] += jnp.sum(
            (grad_normed * scaled).reshape(count // ROWS, ROWS, width), axis=0
        )
        grad_scaled = grad_normed * gains
        scaled_all[pl.ds(j, PAIR)] = grad_scaled.reshape(PAIR, rows, width)
        total = jnp.sum(grad_scaled * mixed, axis=1, keepdims=True)
        cross_wide[pl.ds(slot, PAIR)] = jnp.broadcast_to(total, (count, LANES)).reshape(
            PAIR, rows, LANES
        )

    def send_cross(q):
        at = lax.rem(q, 2) * span
        columns = jnp.zeros((rows, LANES), F32)
        for k in range(span):
            columns = jnp.where(lane == k, cross_wide[at + k], columns)
        exchange(crosses, q, columns, cross_send, cross_recv)

    def back_chunk(q):
        at = lax.rem(q, 2) * span
        inverse = inverse_rows[lax.rem(q, 2)]
        spread(collect(crosses, q, cross_recv) * inverse * inverse * inverse, cross_wide, at)
        for pair in range(span // 2):
            turned = []
            for odd in range(2):
                k = 2 * pair + odd
                j = q * span + k
                wide = jnp.concatenate([inverse_wide[at + k]] * halves, axis=1)
                pull = jnp.concatenate([cross_wide[at + k]] * halves, axis=1)
                grad_mixed = (
                    cotangent[j].astype(F32) + wide * scaled_all[j] - pull * mixed_all[j]
                ).astype(BF16)
                acc_second[...] += dot_columns(moved[j], grad_mixed)
                turned.append(dot(second[...], grad_mixed).reshape(size, local_a, width))
            send_two[:, q * (span // 2) + pair] = jnp.concatenate(turned, axis=1).astype(BF16)

    mix_chunk(0)
    send_far(*first_route(1), start=1)
    send_far(*first_route(2), stop=1)
    send_near(*first_route(2))
    lax.fori_loop(local_j * 3 // 4, local_j, grad_act_rows, 0)

    def chunk(q, carry):
        inverse = lax.rsqrt(collect(squares, q, square_recv) + EPSILON)
        inverse_rows[lax.rem(q, 2)] = inverse
        spread(inverse, inverse_wide, lax.rem(q, 2) * span)

        def tile(step, inner):
            mlp_tile(q, step)

            @pl.when((step == 0) & (q < CHUNKS - 1))
            def _():
                mix_chunk(q + 1)

            @pl.when((step == 0) & (q < CHUNKS - 2))
            def _():
                send_far(*first_route(q + 2), start=1)

            @pl.when((step == 0) & (q < CHUNKS - 3))
            def _():
                send_far(*first_route(q + 3), stop=1)
                send_near(*first_route(q + 3))

            @pl.when((step == 0) & (q > 0))
            def _():
                back_chunk(q - 1)
                send_near(*second_route(q - 1))

            return inner

        lax.fori_loop(0, span // PAIR, tile, 0)
        send_cross(q)

        @pl.when(q > 0)
        def _():
            send_far(*second_route(q - 1))

        return carry

    lax.fori_loop(0, CHUNKS, chunk, 0)

    def pack(target, pieces):
        at = 0
        while pieces:
            joined = pieces.pop(0)
            if joined.shape[1] % 16:
                joined = jnp.concatenate([joined, pieces.pop(0)], axis=1)
            height = joined.shape[1]
            joined = joined.astype(BF16).reshape(size // 2, 2, height, LANES)
            target[:, :, at : at + height, :] = joined
            at += height

    mine = lax.rem(me, 2)
    other = 1 - mine
    mate = me + 1 - 2 * mine
    place = me // 2
    places = size // 2

    def send_mate(source, target, index):
        pltpu.make_async_remote_copy(
            src_ref=source,
            dst_ref=target,
            send_sem=grad_send.at[index],
            recv_sem=grad_recv.at[index],
            device_id={"ctx": mate},
            device_id_type=MESH,
        ).start()

    def send_places(source, target, index):
        def launch(k, carry):
            there = lax.rem(place + STRIDE * k, places)
            pltpu.make_async_remote_copy(
                src_ref=source.at[there],
                dst_ref=target.at[place],
                send_sem=grad_send.at[index],
                recv_sem=grad_recv.at[index],
                device_id={"ctx": 2 * there + mine},
                device_id_type=MESH,
            ).start()
            return carry

        lax.fori_loop(1, places, launch, 0)
        pltpu.make_async_copy(source.at[place], target.at[place], grad_recv.at[index]).start()

    def arrive(got, index):
        pltpu.make_async_copy(got, got, grad_recv.at[index]).wait()

    def add_up(got):
        def add(k, total):
            return total + got[k].astype(F32)

        return lax.fori_loop(0, got.shape[0], add, jnp.zeros(got.shape[1:], F32), unroll=4)

    pack(pack_up, lane_blocks(acc_up[...].reshape(size, width // size, hidden)))

    back_chunk(CHUNKS - 1)
    send_far(*second_route(CHUNKS - 1))
    send_near(*second_route(CHUNKS - 1))
    send_mate(pack_up.at[:, other], got_far, 0)

    seconds = lane_blocks(acc_second[...].reshape(size, local_a, rows))
    downs = lane_blocks((acc_down[...] * 0.5).T.reshape(size, hidden // size, width))
    gain_row = jnp.sum(acc_gain[...], axis=0, keepdims=True)
    gains = [
        jnp.broadcast_to(piece[None], (size, ROWS, LANES)) for piece in lane_blocks(gain_row)
    ]
    pack(pack_rest, seconds + downs + gains)
    send_places(pack_rest, got_rest, 2)

    arrive(got_far, 0)
    pack_near[...] = (pack_up[:, mine].astype(F32) + got_far[...].astype(F32)).astype(BF16)
    send_places(pack_near, got_up, 1)

    chunk_height = span * local_a
    for q in range(CHUNKS):
        arrived = recv_two.at[:, q * (span // 2) : (q + 1) * (span // 2)]
        pltpu.make_async_copy(arrived, arrived, two_recv.at[q]).wait()

        def unpack(k, carry):
            value = recv_two[k, q * (span // 2) : (q + 1) * (span // 2)].astype(F32)
            value = value.reshape(chunk_height, width)
            at = pl.multiple_of(k * local_j * local_a + q * chunk_height, chunk_height)
            for h, piece in enumerate(lane_blocks(value)):
                unpacked[h, pl.ds(at, chunk_height), :] = piece
            return carry

        lax.fori_loop(0, size, unpack, 0, unroll=4)

    def back_row(step, carry):
        for odd in range(2):
            a = step * 2 + odd
            grad_gated = jnp.concatenate(
                [
                    unpacked.at[h][pl.ds(a, positions, stride=local_a), :]
                    for h in range(halves)
                ],
                axis=1,
            )
            inputs = signal[a]
            gate = lax.logistic(inputs.astype(F32))
            opened = grad_gated * gate
            grad_mix = opened.astype(BF16)
            grad_mixes[a] = grad_mix
            first_mix[a] = opened * first_mix[a] * (1.0 - gate)
            acc_first[...] += dot_columns(inputs, grad_mix)
        return carry

    lax.fori_loop(0, local_a // 2, back_row, 0)
    pack_first[...] = acc_first[...].reshape(pack_first.shape).astype(BF16)
    whole = pl.ds(0, pack_first.shape[1])
    route = (pack_first, got_first, whole, grad_send.at[4], grad_recv.at[4])
    send_far(*route)
    send_near(*route)

    arrive(got_rest, 2)
    rest = add_up(got_rest)
    pack_last[...] = jnp.where(mine == 0, rest[1], rest[0]).astype(BF16)
    send_mate(pack_last, got_last, 3)

    def signal_row(a, carry):
        grad_signal[a] = (dot(first[...], grad_mixes[a]) + first_mix[a]).astype(BF16)
        return carry

    lax.fori_loop(0, local_a, signal_row, 0)

    def unfold(out, total, at):
        height = out.shape[0]
        for h in range(out.shape[1] // LANES):
            out[:, h * LANES : (h + 1) * LANES] = total[at : at + height]
            at += height
        return at

    arrive(got_up, 1)
    unfold(out_up, add_up(got_up) * grad_scale, 0)
    arrive(got_last, 3)
    total = jnp.where(mine == 0, rest[0], rest[1])
    total = (total + got_last[...].astype(F32)) * grad_scale
    at = unfold(out_second, total, 0)
    at = unfold(out_down, total, at)
    gain_sum = jnp.concatenate(
        [total[at + h * ROWS : at + (h + 1) * ROWS] for h in range(halves)], axis=1
    )
    turn = lax.rem(width - me * (width // size), width)
    out_gain[...] = pltpu.roll(gain_sum, turn, 1)[:, :LANES]
    arrive(got_first, 4)
    out_first[...] = add_up(got_first) * grad_scale

    def drain(ref, sem):
        pltpu.make_async_copy(ref, ref, sem).wait()

    drain(send_one.at[: size - 1], one_send)
    drain(send_two.at[: size - 1], two_send)
    drain(got_far, grad_send.at[0])
    drain(pack_near.at[: places - 1], grad_send.at[1])
    drain(pack_rest.at[: places - 1], grad_send.at[2])
    drain(pack_last, grad_send.at[3])
    drain(pack_first.at[: size - 1], grad_send.at[4])
    if groups > 1:
        drain(squares.at[:, : groups - 1], square_send)
        drain(crosses.at[:, : groups - 1], cross_send)


def finish(*refs):
    sources, targets, sems = refs[:7], refs[7:14], refs[14]
    copies = [
        pltpu.make_async_copy(sources[k], targets[k], sems.at[k]) for k in range(6)
    ]
    for copy in copies:
        copy.start()
    targets[6][...] = sources[6][:1, : targets[6].shape[1]]
    for copy in copies:
        copy.wait()


def shards(mesh, signal, factor_first, factor_second, up_weight, down_weight, norm_gain, cotangent):
    size, groups = mesh.shape["ctx"], mesh.shape["ch"]
    local_a, positions, width = signal.shape
    local_j, rows, _ = cotangent.shape
    hidden = up_weight.shape[2]
    halves = width // LANES
    span = local_j // CHUNKS
    block = min(128, positions)
    vmem = pl.BlockSpec(memory_space=pltpu.VMEM)
    anywhere = pl.BlockSpec(memory_space=pl.ANY)
    up_rows = width // size * (hidden // LANES)
    rest_rows = local_a * (rows // LANES) + hidden // size * halves + ROWS * halves

    results = (
        (cotangent.shape, BF16),
        (signal.shape, BF16),
        ((positions // size, positions), F32),
        ((rows // size, rows), F32),
        ((width // size, hidden), F32),
        ((hidden // size, width), F32),
    )
    dma = pltpu.SemaphoreType.DMA
    scratch = [
        pltpu.VMEM(signal.shape, BF16),
        pltpu.VMEM((positions, positions), BF16),
        pltpu.VMEM((rows, rows), BF16),
        pltpu.VMEM((width, hidden), BF16),
        pltpu.VMEM((hidden, width), BF16),
        pltpu.VMEM((1, width), F32),
        pltpu.VMEM(cotangent.shape, BF16),
        pltpu.VMEM((positions, positions), BF16),
        pltpu.VMEM((rows, rows), BF16),
        pltpu.VMEM((hidden, width), BF16),
        pltpu.VMEM((width, hidden), BF16),
        pltpu.VMEM((local_a, positions, width), F32),
        pltpu.VMEM((halves, local_a * (block + ROWS), LANES), F32),
        pltpu.VMEM((size, local_j * local_a, width), BF16),
        pltpu.VMEM((size, local_j * local_a, width), BF16),
        pltpu.VMEM((local_j, rows, width), BF16),
        pltpu.VMEM((local_j, rows, width), F32),
        pltpu.VMEM((local_j, rows, width), F32),
        pltpu.VMEM((local_j, rows, hidden), BF16),
        pltpu.VMEM((CHUNKS, groups, ROWS, rows), F32),
        pltpu.VMEM((CHUNKS, groups, ROWS, rows), F32),
        pltpu.VMEM((2, ROWS, rows), F32),
        pltpu.VMEM((2 * span, rows, LANES), F32),
        pltpu.VMEM((2 * span, rows, LANES), F32),
        pltpu.VMEM((size, local_j // 2, 2 * local_a, width), BF16),
        pltpu.VMEM((size, local_j // 2, 2 * local_a, width), BF16),
        pltpu.VMEM((halves, positions * local_a, LANES), F32),
        pltpu.VMEM((width, hidden), F32),
        pltpu.VMEM((width, hidden), F32),
        pltpu.VMEM((rows, rows), F32),
        pltpu.VMEM((positions, positions), F32),
        pltpu.VMEM((ROWS, width), F32),
        pltpu.VMEM(signal.shape, BF16),
        pltpu.VMEM((size // 2, 2, up_rows, LANES), BF16),
        pltpu.VMEM((size // 2, up_rows, LANES), BF16),
        pltpu.VMEM((size // 2, up_rows, LANES), BF16),
        pltpu.VMEM((size // 2, up_rows, LANES), BF16),
        pltpu.VMEM((size // 2, 2, rest_rows, LANES), BF16),
        pltpu.VMEM((size // 2, 2, rest_rows, LANES), BF16),
        pltpu.VMEM((rest_rows, LANES), BF16),
        pltpu.VMEM((rest_rows, LANES), BF16),
        pltpu.VMEM((size, positions // size, positions), BF16),
        pltpu.VMEM((size, positions // size, positions), BF16),
        dma((7,)), dma, dma((CHUNKS,)), dma, dma((CHUNKS,)), dma, dma((CHUNKS,)), dma,
        dma((CHUNKS,)), dma((5,)), dma((5,)),
    ]
    values = pl.pallas_call(
        functools.partial(kernel, groups),
        out_shape=tuple(OUT(*result) for result in results) + (OUT((ROWS, LANES), F32),),
        in_specs=[anywhere] * 7,
        out_specs=(vmem,) * 7,
        scratch_shapes=scratch,
        compiler_params=pltpu.CompilerParams(
            collective_id=0, has_side_effects=True, vmem_limit_bytes=LIMIT
        ),
    )(signal, factor_first[0], factor_second[0], up_weight[0], down_weight[0], norm_gain, cotangent)
    shapes = [jax.ShapeDtypeStruct(*result) for result in results]
    values = pl.pallas_call(
        finish,
        out_shape=(*shapes, jax.ShapeDtypeStruct((1, width // size), F32)),
        in_specs=[vmem] * 7,
        out_specs=(anywhere,) * 6 + (vmem,),
        scratch_shapes=[dma((6,))],
        compiler_params=pltpu.CompilerParams(vmem_limit_bytes=4194304),
    )(*[pltpu.with_memory_space_constraint(value, pltpu.VMEM) for value in values])
    return (*values[:2], *(value[None] for value in values[2:6]), values[6])


def solution(mesh):
    placed = (
        P("ctx", None, "ch"),
        P("ch", None, None),
        P("ch", None, None),
        P("ch", None, None),
        P("ch", None, None),
        P("ch", None),
        P("ctx", None, "ch"),
    )
    return jax.shard_map(
        functools.partial(shards, mesh),
        mesh=mesh,
        in_specs=placed,
        out_specs=(
            P("ctx", None, "ch"),
            P("ctx", None, "ch"),
            P("ch", "ctx", None),
            P("ch", "ctx", None),
            P("ch", "ctx", None),
            P("ch", "ctx", None),
            P("ch", "ctx"),
        ),
        check_vma=False,
    )
```

```python
import functools
import math

import jax
import jax.numpy as jnp
from jax import lax
from jax.experimental import pallas as pl
from jax.experimental.pallas import tpu as pltpu
from jax.sharding import PartitionSpec as P

D = 1024
EPSILON = 1e-05
CHUNKS = 4
LANES = 128
ROWS = 8
HIDDEN = 256
PAIR = 2
STRIDE = 5
MESH = pl.DeviceIdType.MESH
BF16 = jnp.bfloat16
F32 = jnp.float32
CUBIC = 0.044715
SLOPE = math.sqrt(2.0 / math.pi)


def dot(lhs, rhs):
    return jnp.dot(lhs, rhs, preferred_element_type=F32)


def dot_rows(lhs, rhs):
    return lax.dot_general(lhs, rhs, (((0,), (0,)), ((), ())), preferred_element_type=F32)


def dot_columns(lhs, rhs):
    return lax.dot_general(lhs, rhs, (((1,), (1,)), ((), ())), preferred_element_type=F32)


def lane_blocks(value):
    return [value[..., at : at + LANES] for at in range(0, value.shape[-1], LANES)]


OUT = pltpu.VMEM
LIMIT = 61865984

def kernel(
    groups, signal_in, first_in, second_in, up_in, down_in, gain_in, cotangent_in,
    layer_out, grad_signal, out_first, out_second, out_up, out_down, out_gain,
    signal, first, second, up, down, gain, cotangent,
    first_t, second_t, up_t, down_t, first_mix, stage, send_one, recv_one, moved, mixed_all,
    scaled_all, grad_acts, squares, crosses, inverse_rows, inverse_wide, cross_wide, send_two,
    recv_two, unpacked, acc_up, acc_down, acc_second, acc_first, acc_gain, grad_mixes, pack_up,
    got_far, pack_near, got_up, pack_rest, got_rest, pack_last, got_last, pack_first, got_first, load_sem, one_send, one_recv, two_send, two_recv,
    square_send, square_recv, cross_send, cross_recv, grad_send, grad_recv,
):
    me = lax.axis_index("ctx")
    channel = lax.axis_index("ch")
    local_a, positions, width = signal.shape
    local_j, rows, _ = cotangent.shape
    hidden = up.shape[1]
    size = rows // local_a
    span = local_j // CHUNKS
    block = stage.shape[1] // local_a - ROWS
    per_block = block // local_j
    blocks = positions // block
    pitch = block + ROWS
    chunk_rows = span * local_a
    halves = width // LANES
    grad_scale = 1.0 / math.sqrt(rows * positions)

    loads = [
        pltpu.make_async_copy(source, target, load_sem.at[k])
        for k, (source, target) in enumerate(
            zip(
                (first_in, signal_in, second_in, up_in, down_in, gain_in, cotangent_in),
                (first, signal, second, up, down, gain, cotangent),
            )
        )
    ]
    for load in loads[:2]:
        load.start()

    barrier = pltpu.get_barrier_semaphore()

    def greet(k, carry):
        pl.semaphore_signal(
            barrier,
            inc=1,
            device_id={"ctx": lax.rem(me + 1 + lax.rem(k + size // 2 + 2, size - 1), size)},
            device_id_type=MESH,
        )
        return carry

    lax.fori_loop(1, size, greet, 0)
    for k in range(1, groups):
        pl.semaphore_signal(
            barrier, inc=1, device_id={"ch": lax.rem(channel + k, groups)}, device_id_type=MESH
        )

    loads[0].wait()
    first_t[...] = first[...].T
    loads[1].wait()
    for load in loads[2:]:
        load.start()

    def first_block(at, carry):
        part = pl.ds(pl.multiple_of(at * block, block), block)
        weights = first_t[part, :]
        for a in range(local_a):
            mix = dot(weights, signal[a])
            first_mix[a, part, :] = mix
            gated = mix * lax.logistic(signal[a, part, :].astype(F32))
            for h, piece in enumerate(lane_blocks(gated)):
                stage[h, a * pitch : a * pitch + block, :] = piece

        def turn(k, inner):
            for h in range(halves):
                taken = [
                    stage.at[h][pl.ds(k * local_j + j, local_a, stride=pitch), :]
                    for j in range(local_j)
                ]
                send_one[at * per_block + k, :, h * LANES : (h + 1) * LANES] = jnp.concatenate(
                    taken, axis=0
                ).astype(BF16)
            return inner

        lax.fori_loop(0, per_block, turn, 0)
        return carry

    lax.fori_loop(0, blocks, first_block, 0)
    pl.semaphore_wait(barrier, size - 1 + groups - 1)

    half = size // 4

    def send_part(source, target, part, send_sem, recv_sem, odd, start, stop):
        def launch(k, carry):
            peer = lax.rem(me + 2 * lax.rem(STRIDE * k, size // 2) + odd, size)
            pltpu.make_async_remote_copy(
                src_ref=source.at[peer, part],
                dst_ref=target.at[me, part],
                send_sem=send_sem,
                recv_sem=recv_sem,
                device_id={"ctx": peer},
                device_id_type=MESH,
            ).start()
            return carry

        lax.fori_loop(start, stop, launch, 0)

    def send_near(source, target, part, send_sem, recv_sem):
        send_part(source, target, part, send_sem, recv_sem, 0, 1, 2 * half)
        pltpu.make_async_copy(source.at[me, part], target.at[me, part], recv_sem).start()

    def send_far(*route, start=0, stop=2):
        send_part(*route, 1, start * half, stop * half)

    def first_route(q):
        part = pl.ds(pl.multiple_of(q * chunk_rows, chunk_rows), chunk_rows)
        return send_one, recv_one, part, one_send, one_recv.at[q]

    def second_route(q):
        part = pl.ds(q * (span // 2), span // 2)
        return send_two, recv_two, part, two_send, two_recv.at[q]

    send_far(*first_route(0))
    send_near(*first_route(0))
    send_far(*first_route(1), stop=1)
    send_near(*first_route(1))
    for load in loads[2:]:
        load.wait()
    second_t[...] = second[...].T
    up_t[...] = up[...].T
    down[...] = (down[...].astype(F32) * 0.5).astype(BF16)
    down_t[...] = down[...].T
    acc_up[...] = jnp.zeros_like(acc_up)
    acc_down[...] = jnp.zeros_like(acc_down)
    acc_second[...] = jnp.zeros_like(acc_second)
    acc_first[...] = jnp.zeros_like(acc_first)
    acc_gain[...] = jnp.zeros_like(acc_gain)

    def grad_act_rows(j, carry):
        grad_acts[j] = dot(cotangent[j], down_t[...]).astype(BF16)
        return carry

    lax.fori_loop(0, local_j * 3 // 4, grad_act_rows, 0)

    lane = lax.broadcasted_iota(jnp.int32, (rows, LANES), 1)

    def exchange(table, q, columns, send_sem, recv_sem):
        table[q, channel] = columns.T[:ROWS]
        for k in range(1, groups):
            pltpu.make_async_remote_copy(
                src_ref=table.at[q, channel],
                dst_ref=table.at[q, channel],
                send_sem=send_sem,
                recv_sem=recv_sem.at[q],
                device_id={"ch": lax.rem(channel + k, groups)},
                device_id_type=MESH,
            ).start()

    def collect(table, q, recv_sem):
        if groups > 1:
            others = table.at[q, : groups - 1]
            pltpu.make_async_copy(others, others, recv_sem.at[q]).wait()
        total = table[q, 0]
        for k in range(1, groups):
            total = total + table[q, k]
        return total / D

    def spread(values, wide, at):
        tall = jnp.concatenate([values] * (LANES // ROWS), axis=0).T
        for k in range(span):
            wide[at + k] = jnp.broadcast_to(tall[:, k : k + 1], (rows, LANES))

    def mix_chunk(q):
        part = pl.ds(pl.multiple_of(q * chunk_rows, chunk_rows), chunk_rows)
        arrived = recv_one.at[:, part]
        pltpu.make_async_copy(arrived, arrived, one_recv.at[q]).wait()
        columns = jnp.zeros((rows, LANES), F32)
        for pair in range(span // 2):
            at = pl.multiple_of(q * chunk_rows + pair * 2 * local_a, 2 * local_a)
            both = recv_one[:, pl.ds(at, 2 * local_a), :].astype(F32)
            for odd in range(2):
                k = 2 * pair + odd
                rows_k = both[:, odd * local_a : (odd + 1) * local_a, :]
                rows_k = rows_k.reshape(rows, width).astype(BF16)
                moved[q * span + k] = rows_k
                mixed = dot(second_t[...], rows_k)
                mixed_all[q * span + k] = mixed
                total = jnp.sum(mixed * mixed, axis=1, keepdims=True)
                columns = jnp.where(lane == k, total, columns)
        exchange(squares, q, columns, square_send, square_recv)

    def mlp_tile(q, step):
        j = q * span + step * PAIR
        slot = lax.rem(q, 2) * span + step * PAIR
        count = PAIR * rows
        mixed = mixed_all[pl.ds(j, PAIR)].reshape(count, width)
        wide = inverse_wide[pl.ds(slot, PAIR)].reshape(count, LANES)
        scaled = mixed * jnp.concatenate([wide] * halves, axis=1)
        gains = gain[...]
        normed = (scaled * gains).astype(BF16)
        upstream = cotangent[pl.ds(j, PAIR)].reshape(count, width)
        out = mixed
        grad_normed = None
        parts = [slice(at, at + HIDDEN) for at in range(0, hidden, HIDDEN)]
        queue = [dot(normed, up[:, parts[0]]), dot(normed, up[:, parts[1]])]
        for n, part in enumerate(parts):
            pre = queue.pop(0)
            if n + 2 < len(parts):
                queue.append(dot(normed, up[:, parts[n + 2]]))
            grad_act = grad_acts[pl.ds(j, PAIR), :, part].reshape(count, HIDDEN).astype(F32)
            base = SLOPE + (SLOPE * CUBIC) * (pre * pre)
            curve = jnp.tanh(pre * base)
            opened = 1.0 + curve
            act = (pre * opened).astype(BF16)
            bend = pre * (3.0 * base - 2.0 * SLOPE)
            grad_pre = (grad_act * (opened * (1.0 + (1.0 - curve) * bend))).astype(BF16)
            out = out + dot(act, down[part, :])
            back = dot(grad_pre, up_t[part, :])
            grad_normed = back if grad_normed is None else grad_normed + back
            acc_down[:, part] += dot_rows(upstream, act)
            acc_up[:, part] += dot_rows(normed, grad_pre)
        layer_out[pl.ds(j, PAIR)] = out.astype(BF16).reshape(PAIR, rows, width)
        acc_gain[...] += jnp.sum(
            (grad_normed * scaled).reshape(count // ROWS, ROWS, width), axis=0
        )
        grad_scaled = grad_normed * gains
        scaled_all[pl.ds(j, PAIR)] = grad_scaled.reshape(PAIR, rows, width)
        total = jnp.sum(grad_scaled * mixed, axis=1, keepdims=True)
        cross_wide[pl.ds(slot, PAIR)] = jnp.broadcast_to(total, (count, LANES)).reshape(
            PAIR, rows, LANES
        )

    def send_cross(q):
        at = lax.rem(q, 2) * span
        columns = jnp.zeros((rows, LANES), F32)
        for k in range(span):
            columns = jnp.where(lane == k, cross_wide[at + k], columns)
        exchange(crosses, q, columns, cross_send, cross_recv)

    def back_chunk(q):
        at = lax.rem(q, 2) * span
        inverse = inverse_rows[lax.rem(q, 2)]
        spread(collect(crosses, q, cross_recv) * inverse * inverse * inverse, cross_wide, at)
        for pair in range(span // 2):
            turned = []
            for odd in range(2):
                k = 2 * pair + odd
                j = q * span + k
                wide = jnp.concatenate([inverse_wide[at + k]] * halves, axis=1)
                pull = jnp.concatenate([cross_wide[at + k]] * halves, axis=1)
                grad_mixed = (
                    cotangent[j].astype(F32) + wide * scaled_all[j] - pull * mixed_all[j]
                ).astype(BF16)
                acc_second[...] += dot_columns(moved[j], grad_mixed)
                turned.append(dot(second[...], grad_mixed).reshape(size, local_a, width))
            send_two[:, q * (span // 2) + pair] = jnp.concatenate(turned, axis=1).astype(BF16)

    mix_chunk(0)
    send_far(*first_route(1), start=1)
    send_far(*first_route(2), stop=1)
    send_near(*first_route(2))
    lax.fori_loop(local_j * 3 // 4, local_j, grad_act_rows, 0)

    def chunk(q, carry):
        inverse = lax.rsqrt(collect(squares, q, square_recv) + EPSILON)
        inverse_rows[lax.rem(q, 2)] = inverse
        spread(inverse, inverse_wide, lax.rem(q, 2) * span)

        def tile(step, inner):
            mlp_tile(q, step)

            @pl.when((step == 0) & (q < CHUNKS - 1))
            def _():
                mix_chunk(q + 1)

            @pl.when((step == 0) & (q < CHUNKS - 2))
            def _():
                send_far(*first_route(q + 2), start=1)

            @pl.when((step == 0) & (q < CHUNKS - 3))
            def _():
                send_far(*first_route(q + 3), stop=1)
                send_near(*first_route(q + 3))

            return inner

        lax.fori_loop(0, span // PAIR, tile, 0)
        send_cross(q)

        @pl.when(q > 0)
        def _():
            back_chunk(q - 1)
            send_far(*second_route(q - 1))
            send_near(*second_route(q - 1))

        return carry

    lax.fori_loop(0, CHUNKS, chunk, 0)

    def pack(target, pieces):
        at = 0
        while pieces:
            joined = pieces.pop(0)
            if joined.shape[1] % 16:
                joined = jnp.concatenate([joined, pieces.pop(0)], axis=1)
            height = joined.shape[1]
            joined = joined.astype(BF16).reshape(size // 2, 2, height, LANES)
            target[:, :, at : at + height, :] = joined
            at += height

    mine = lax.rem(me, 2)
    other = 1 - mine
    mate = me + 1 - 2 * mine
    place = me // 2
    places = size // 2

    def send_mate(source, target, index):
        pltpu.make_async_remote_copy(
            src_ref=source,
            dst_ref=target,
            send_sem=grad_send.at[index],
            recv_sem=grad_recv.at[index],
            device_id={"ctx": mate},
            device_id_type=MESH,
        ).start()

    def send_places(source, target, index):
        def launch(k, carry):
            there = lax.rem(place + STRIDE * k, places)
            pltpu.make_async_remote_copy(
                src_ref=source.at[there],
                dst_ref=target.at[place],
                send_sem=grad_send.at[index],
                recv_sem=grad_recv.at[index],
                device_id={"ctx": 2 * there + mine},
                device_id_type=MESH,
            ).start()
            return carry

        lax.fori_loop(1, places, launch, 0)
        pltpu.make_async_copy(source.at[place], target.at[place], grad_recv.at[index]).start()

    def arrive(got, index):
        pltpu.make_async_copy(got, got, grad_recv.at[index]).wait()

    def add_up(got):
        def add(k, total):
            return total + got[k].astype(F32)

        return lax.fori_loop(0, got.shape[0], add, jnp.zeros(got.shape[1:], F32), unroll=4)

    pack(pack_up, lane_blocks(acc_up[...].reshape(size, width // size, hidden)))

    back_chunk(CHUNKS - 1)
    send_far(*second_route(CHUNKS - 1))
    send_near(*second_route(CHUNKS - 1))
    send_mate(pack_up.at[:, other], got_far, 0)

    seconds = lane_blocks(acc_second[...].reshape(size, local_a, rows))
    downs = lane_blocks((acc_down[...] * 0.5).T.reshape(size, hidden // size, width))
    gain_row = jnp.sum(acc_gain[...], axis=0, keepdims=True)
    gains = [
        jnp.broadcast_to(piece[None], (size, ROWS, LANES)) for piece in lane_blocks(gain_row)
    ]
    pack(pack_rest, seconds + downs + gains)
    send_places(pack_rest, got_rest, 2)

    arrive(got_far, 0)
    pack_near[...] = (pack_up[:, mine].astype(F32) + got_far[...].astype(F32)).astype(BF16)
    send_places(pack_near, got_up, 1)

    chunk_height = span * local_a
    for q in range(CHUNKS):
        arrived = recv_two.at[:, q * (span // 2) : (q + 1) * (span // 2)]
        pltpu.make_async_copy(arrived, arrived, two_recv.at[q]).wait()

        def unpack(k, carry):
            value = recv_two[k, q * (span // 2) : (q + 1) * (span // 2)].astype(F32)
            value = value.reshape(chunk_height, width)
            at = pl.multiple_of(k * local_j * local_a + q * chunk_height, chunk_height)
            for h, piece in enumerate(lane_blocks(value)):
                unpacked[h, pl.ds(at, chunk_height), :] = piece
            return carry

        lax.fori_loop(0, size, unpack, 0, unroll=4)

    def back_row(step, carry):
        for odd in range(2):
            a = step * 2 + odd
            grad_gated = jnp.concatenate(
                [
                    unpacked.at[h][pl.ds(a, positions, stride=local_a), :]
                    for h in range(halves)
                ],
                axis=1,
            )
            inputs = signal[a]
            gate = lax.logistic(inputs.astype(F32))
            opened = grad_gated * gate
            grad_mix = opened.astype(BF16)
            grad_mixes[a] = grad_mix
            first_mix[a] = opened * first_mix[a] * (1.0 - gate)
            acc_first[...] += dot_columns(inputs, grad_mix)
        return carry

    lax.fori_loop(0, local_a // 2, back_row, 0)
    pack_first[...] = acc_first[...].reshape(pack_first.shape).astype(BF16)
    whole = pl.ds(0, pack_first.shape[1])
    route = (pack_first, got_first, whole, grad_send.at[4], grad_recv.at[4])
    send_far(*route)
    send_near(*route)

    arrive(got_rest, 2)
    rest = add_up(got_rest)
    pack_last[...] = jnp.where(mine == 0, rest[1], rest[0]).astype(BF16)
    send_mate(pack_last, got_last, 3)

    def signal_row(a, carry):
        grad_signal[a] = (dot(first[...], grad_mixes[a]) + first_mix[a]).astype(BF16)
        return carry

    lax.fori_loop(0, local_a, signal_row, 0)

    def unfold(out, total, at):
        height = out.shape[0]
        for h in range(out.shape[1] // LANES):
            out[:, h * LANES : (h + 1) * LANES] = total[at : at + height]
            at += height
        return at

    arrive(got_up, 1)
    unfold(out_up, add_up(got_up) * grad_scale, 0)
    arrive(got_last, 3)
    total = jnp.where(mine == 0, rest[0], rest[1])
    total = (total + got_last[...].astype(F32)) * grad_scale
    at = unfold(out_second, total, 0)
    at = unfold(out_down, total, at)
    gain_sum = jnp.concatenate(
        [total[at + h * ROWS : at + (h + 1) * ROWS] for h in range(halves)], axis=1
    )
    turn = lax.rem(width - me * (width // size), width)
    out_gain[...] = pltpu.roll(gain_sum, turn, 1)[:, :LANES]
    arrive(got_first, 4)
    out_first[...] = add_up(got_first) * grad_scale

    def drain(ref, sem):
        pltpu.make_async_copy(ref, ref, sem).wait()

    drain(send_one.at[: size - 1], one_send)
    drain(send_two.at[: size - 1], two_send)
    drain(got_far, grad_send.at[0])
    drain(pack_near.at[: places - 1], grad_send.at[1])
    drain(pack_rest.at[: places - 1], grad_send.at[2])
    drain(pack_last, grad_send.at[3])
    drain(pack_first.at[: size - 1], grad_send.at[4])
    if groups > 1:
        drain(squares.at[:, : groups - 1], square_send)
        drain(crosses.at[:, : groups - 1], cross_send)


def finish(*refs):
    sources, targets, sems = refs[:7], refs[7:14], refs[14]
    copies = [
        pltpu.make_async_copy(sources[k], targets[k], sems.at[k]) for k in range(6)
    ]
    for copy in copies:
        copy.start()
    targets[6][...] = sources[6][:1, : targets[6].shape[1]]
    for copy in copies:
        copy.wait()


def shards(mesh, signal, factor_first, factor_second, up_weight, down_weight, norm_gain, cotangent):
    size, groups = mesh.shape["ctx"], mesh.shape["ch"]
    local_a, positions, width = signal.shape
    local_j, rows, _ = cotangent.shape
    hidden = up_weight.shape[2]
    halves = width // LANES
    span = local_j // CHUNKS
    block = min(128, positions)
    vmem = pl.BlockSpec(memory_space=pltpu.VMEM)
    anywhere = pl.BlockSpec(memory_space=pl.ANY)
    up_rows = width // size * (hidden // LANES)
    rest_rows = local_a * (rows // LANES) + hidden // size * halves + ROWS * halves

    results = (
        (cotangent.shape, BF16),
        (signal.shape, BF16),
        ((positions // size, positions), F32),
        ((rows // size, rows), F32),
        ((width // size, hidden), F32),
        ((hidden // size, width), F32),
    )
    dma = pltpu.SemaphoreType.DMA
    scratch = [
        pltpu.VMEM(signal.shape, BF16),
        pltpu.VMEM((positions, positions), BF16),
        pltpu.VMEM((rows, rows), BF16),
        pltpu.VMEM((width, hidden), BF16),
        pltpu.VMEM((hidden, width), BF16),
        pltpu.VMEM((1, width), F32),
        pltpu.VMEM(cotangent.shape, BF16),
        pltpu.VMEM((positions, positions), BF16),
        pltpu.VMEM((rows, rows), BF16),
        pltpu.VMEM((hidden, width), BF16),
        pltpu.VMEM((width, hidden), BF16),
        pltpu.VMEM((local_a, positions, width), F32),
        pltpu.VMEM((halves, local_a * (block + ROWS), LANES), F32),
        pltpu.VMEM((size, local_j * local_a, width), BF16),
        pltpu.VMEM((size, local_j * local_a, width), BF16),
        pltpu.VMEM((local_j, rows, width), BF16),
        pltpu.VMEM((local_j, rows, width), F32),
        pltpu.VMEM((local_j, rows, width), F32),
        pltpu.VMEM((local_j, rows, hidden), BF16),
        pltpu.VMEM((CHUNKS, groups, ROWS, rows), F32),
        pltpu.VMEM((CHUNKS, groups, ROWS, rows), F32),
        pltpu.VMEM((2, ROWS, rows), F32),
        pltpu.VMEM((2 * span, rows, LANES), F32),
        pltpu.VMEM((2 * span, rows, LANES), F32),
        pltpu.VMEM((size, local_j // 2, 2 * local_a, width), BF16),
        pltpu.VMEM((size, local_j // 2, 2 * local_a, width), BF16),
        pltpu.VMEM((halves, positions * local_a, LANES), F32),
        pltpu.VMEM((width, hidden), F32),
        pltpu.VMEM((width, hidden), F32),
        pltpu.VMEM((rows, rows), F32),
        pltpu.VMEM((positions, positions), F32),
        pltpu.VMEM((ROWS, width), F32),
        pltpu.VMEM(signal.shape, BF16),
        pltpu.VMEM((size // 2, 2, up_rows, LANES), BF16),
        pltpu.VMEM((size // 2, up_rows, LANES), BF16),
        pltpu.VMEM((size // 2, up_rows, LANES), BF16),
        pltpu.VMEM((size // 2, up_rows, LANES), BF16),
        pltpu.VMEM((size // 2, 2, rest_rows, LANES), BF16),
        pltpu.VMEM((size // 2, 2, rest_rows, LANES), BF16),
        pltpu.VMEM((rest_rows, LANES), BF16),
        pltpu.VMEM((rest_rows, LANES), BF16),
        pltpu.VMEM((size, positions // size, positions), BF16),
        pltpu.VMEM((size, positions // size, positions), BF16),
        dma((7,)), dma, dma((CHUNKS,)), dma, dma((CHUNKS,)), dma, dma((CHUNKS,)), dma,
        dma((CHUNKS,)), dma((5,)), dma((5,)),
    ]
    values = pl.pallas_call(
        functools.partial(kernel, groups),
        out_shape=tuple(OUT(*result) for result in results) + (OUT((ROWS, LANES), F32),),
        in_specs=[anywhere] * 7,
        out_specs=(vmem,) * 7,
        scratch_shapes=scratch,
        compiler_params=pltpu.CompilerParams(
            collective_id=0, has_side_effects=True, vmem_limit_bytes=LIMIT
        ),
    )(signal, factor_first[0], factor_second[0], up_weight[0], down_weight[0], norm_gain, cotangent)
    shapes = [jax.ShapeDtypeStruct(*result) for result in results]
    values = pl.pallas_call(
        finish,
        out_shape=(*shapes, jax.ShapeDtypeStruct((1, width // size), F32)),
        in_specs=[vmem] * 7,
        out_specs=(anywhere,) * 6 + (vmem,),
        scratch_shapes=[dma((6,))],
        compiler_params=pltpu.CompilerParams(vmem_limit_bytes=4194304),
    )(*[pltpu.with_memory_space_constraint(value, pltpu.VMEM) for value in values])
    return (*values[:2], *(value[None] for value in values[2:6]), values[6])


def solution(mesh):
    placed = (
        P("ctx", None, "ch"),
        P("ch", None, None),
        P("ch", None, None),
        P("ch", None, None),
        P("ch", None, None),
        P("ch", None),
        P("ctx", None, "ch"),
    )
    return jax.shard_map(
        functools.partial(shards, mesh),
        mesh=mesh,
        in_specs=placed,
        out_specs=(
            P("ctx", None, "ch"),
            P("ctx", None, "ch"),
            P("ch", "ctx", None),
            P("ch", "ctx", None),
            P("ch", "ctx", None),
            P("ch", "ctx", None),
            P("ch", "ctx"),
        ),
        check_vma=False,
    )
```
